32 devices in a mesh: dp: 8 (over y, x, core), vocab: 4 (over z).
Axes of the slice: x: 2, y: 2, z: 4, core: 2. Of those that a mesh axis runs over, the one named last changes fastest.
Arguments:
- student_hidden: bfloat16 [1024, 1536], P('dp'), may hold values from -16 to 16
- head_weight: bfloat16 [1536, 16384], P('dp', 'vocab'), may hold values from -1 to 1
- teacher_logprobs: float32 [1024, 20480], P('dp', 'vocab'), may hold values from -45 to 0, as said below
- align_index: int32 [128, 2], replicated, may hold values from 0 to 159, as said below
- align_tiles: bfloat16 [128, 2, 128, 128], P('vocab'), may hold values from 0 to 6.1
- grad_scale: float32 [1024], P('dp'), may hold values from 30 to 300
Outputs:
- hidden_grad: bfloat16 [1024, 1536], P('dp', 'vocab')
- head_grad: bfloat16 [1536, 16384], P('dp', 'vocab')
The draws below stay inside these ranges and needn't reach their ends.
Inputs may be any that keep to these rules, and one draw needn't show every extreme that they name: `teacher_logprobs`: each row's exponentials sum to 1 over the 20480 teacher entries. `align_index`: teacher block j is held by vocab index j // 40. Of the 64 entries of the student blocks held by one vocab index, at most 32 name teacher blocks held by any one vocab index, and for every vocab index some vocab index holds exactly 32 of them.
All inputs are finite; a program needn't handle non-finite values.
Results may differ from the reference program's by a relative error of at most 0.015.
Values may be sent and summed in bfloat16 or wider, within the bound.
No kernel may reach another device: no remote copies, remote signals or barrier semaphores. Data moves between devices by JAX's collectives and lax.ppermute only.
A program may use at most 128 MiB of HBM per device.

```python
import math
import jax
import jax.numpy as jnp
from jax import lax

D = 1536
BLOCK = 128
K = 2
TOK_DEV = 128
TOKENS = 1024
V_S = 16384
V_T = 20480
NBT_DEV = 40
NB_S = 128
NB_T = 160
PAIRS = 64
CAP = 32
N_DP = 8
N_VOCAB = 4


def shared_head(key):
    folded = jax.random.fold_in(key, 101)
    normal_key = jax.random.fold_in(folded, 0)
    base = jax.random.truncated_normal(normal_key, -6.0, 6.0, (D, V_S), jnp.float32)
    columns = jnp.arange(V_S)
    spread = 1.6 + 0.8 * columns.astype(jnp.float32) / V_S
    weight = jnp.clip(base * spread[None, :] / math.sqrt(D), -1.0, 1.0)
    return weight


def draw_head_weight(key, part):
    weight = shared_head(key)
    return weight.astype(jnp.bfloat16)


def draw_student_hidden(key, part):
    folded = jax.random.fold_in(key, 202)
    row_key = jax.random.fold_in(folded, 0)
    states = 0.5 * jnp.clip(jax.random.normal(row_key, (TOKENS, D), jnp.float32), -8.0, 8.0)
    return states.astype(jnp.bfloat16)


def draw_teacher_logprobs(key, part):
    folded = jax.random.fold_in(key, 303)
    value_key = jax.random.fold_in(folded, 0)
    scores = 0.7 * jax.random.truncated_normal(value_key, -6.0, 6.0, (TOKENS, V_T), jnp.float32)
    return jax.nn.log_softmax(scores, axis=1)


def draw_align_tiles(key, part):
    folded = jax.random.fold_in(key, 404)
    off_key, diag_key = jax.random.split(folded)
    level = 1.0 + 2.0 * jnp.arange(NB_S, dtype=jnp.float32) / NB_S
    off_part = jax.random.uniform(off_key, (NB_S, K, BLOCK, BLOCK), jnp.float32, 0.0, 1.0 / BLOCK)
    diagonal = jax.random.uniform(diag_key, (NB_S, K, BLOCK), jnp.float32, 0.5, 1.5)
    identity = jnp.eye(BLOCK, dtype=jnp.float32)
    tiles = level[:, None, None, None] * (off_part + diagonal[..., None] * identity)
    return tiles.astype(jnp.bfloat16)


def draw_align_index(key, part):
    folded = jax.random.fold_in(key, 505)
    offset_key, rows_key = jax.random.split(folded)
    hot_offset = jax.random.randint(offset_key, (N_VOCAB,), 0, NBT_DEV)

    def one_requester(row_key):
        pick_key, second_key, count_key, order_key, block_key = jax.random.split(row_key, 5)
        leader = jax.random.randint(pick_key, (), 0, N_VOCAB)
        runner = (leader + 1 + jax.random.randint(second_key, (), 0, N_VOCAB - 1)) % N_VOCAB
        runner_count = jax.random.randint(count_key, (), 1, min(CAP, PAIRS - CAP) + 1)
        owners = jnp.arange(N_VOCAB)
        taken = ((owners == leader) | (owners == runner)).astype(jnp.int32)
        others = jnp.argsort(taken * N_VOCAB + owners, stable=True)
        slots = jnp.arange(PAIRS)
        spread_slot = jnp.maximum(slots - CAP - runner_count, 0) % (N_VOCAB - 2)
        owner_of = jnp.where(slots < CAP, leader, jnp.where(slots < CAP + runner_count, runner, others[spread_slot]))
        owner_of = owner_of[jax.random.permutation(order_key, PAIRS)]
        uniform_block = jax.random.randint(block_key, (PAIRS,), 0, NBT_DEV)
        local_block = (uniform_block * uniform_block // NBT_DEV + hot_offset[owner_of]) % NBT_DEV
        return owner_of * NBT_DEV + local_block
    table = jax.vmap(one_requester)(jax.random.split(rows_key, N_VOCAB))
    return table.reshape(NB_S, K).astype(jnp.int32)


def steps_of(own_key, shape, pieces, low, top_value):
    def one(axis_at, shards_of):
        heights = jax.random.uniform(jax.random.fold_in(jax.random.fold_in(own_key, 6), axis_at), (shards_of,), jnp.float32, low / len(pieces), top_value / len(pieces))
        return jnp.repeat(jnp.exp(heights), shape[axis_at] // shards_of).reshape((-1,) + (1,) * (len(shape) - axis_at - 1))

    gain = one(*pieces[0])
    for cut in pieces[1:]:
        gain = gain * one(*cut)
    return gain


def setup_inputs(seed: int = 0) -> dict:
    splits = jax.random.split(jax.random.key(seed), 7)
    student_hidden = draw_student_hidden(jax.random.fold_in(splits[6], 71), 0)
    head_weight = draw_head_weight(jax.random.fold_in(splits[6], 71), 0)
    teacher_logprobs = draw_teacher_logprobs(jax.random.fold_in(splits[6], 71), 0)
    align_index = draw_align_index(jax.random.fold_in(splits[6], 71), 0)
    align_tiles = draw_align_tiles(jax.random.fold_in(splits[6], 71), 0)
    grad_scale = jnp.clip(jnp.exp(math.log(300.0) - 2.3025851 * jax.random.uniform(splits[5], (TOKENS,), jnp.float32) ** steps_of(splits[5], (TOKENS,), ((0, 8),), -0.2, 0.2)), 30.0, 300.0)
    return dict(student_hidden=student_hidden, head_weight=head_weight, teacher_logprobs=teacher_logprobs, align_index=align_index, align_tiles=align_tiles, grad_scale=grad_scale)


def reference(student_hidden, head_weight, teacher_logprobs, align_index, align_tiles, grad_scale):
    hidden_groups = student_hidden.reshape(N_DP, TOK_DEV, D)
    teacher_groups = teacher_logprobs.reshape(N_DP, TOK_DEV, V_T)
    scale_groups = grad_scale.reshape(N_DP, TOK_DEV)
    tiles_wide = align_tiles.astype(jnp.float32)
    flat_index = align_index.reshape(-1).astype(jnp.int32)

    def group_step(head_total, inputs):
        hidden_rows, teacher_rows, scale_rows = inputs
        logits = jnp.dot(hidden_rows, head_weight, preferred_element_type=jnp.float32)
        row_max = jnp.max(logits, axis=1, keepdims=True)
        shifted = jnp.exp(logits - row_max)
        row_total = jnp.sum(shifted, axis=1, keepdims=True)
        student_probs = shifted / row_total
        teacher_low = jnp.exp(teacher_rows).astype(jnp.bfloat16)
        teacher_low = lax.optimization_barrier(teacher_low)
        teacher_probs = teacher_low.astype(jnp.float32).reshape(TOK_DEV, NB_T, BLOCK)
        picked = jnp.take(teacher_probs, flat_index, axis=1).reshape(TOK_DEV, NB_S, K, BLOCK)
        mapped = jnp.einsum("tbkj,bkji->tbi", picked, tiles_wide).reshape(TOK_DEV, V_S)
        mass = jnp.sum(mapped, axis=1, keepdims=True)
        dlogits = (scale_rows[:, None] * (mass * student_probs - mapped)).astype(jnp.bfloat16)
        hidden_part = lax.dot_general(dlogits, head_weight, (((1,), (1,)), ((), ())), preferred_element_type=jnp.float32).astype(jnp.bfloat16)
        head_part = lax.dot_general(hidden_rows, dlogits, (((0,), (0,)), ((), ())), preferred_element_type=jnp.float32).astype(jnp.bfloat16)
        head_part = lax.optimization_barrier(head_part)
        return head_total + head_part.astype(jnp.float32), hidden_part

    head_total, hidden_parts = lax.scan(group_step, jnp.zeros((D, V_S), jnp.float32), (hidden_groups, teacher_groups, scale_groups))
    return hidden_parts.reshape(TOKENS, D), head_total.astype(jnp.bfloat16)
```

```python
import jax
import jax.numpy as jnp
from jax import lax
from jax.sharding import PartitionSpec as P

BLOCK = 128
K = 2


def pair_tables(index_rows, teacher_count, vocab_count):
    owner_of = index_rows // teacher_count
    local_block = index_rows % teacher_count
    onehot = (owner_of[..., None] == jnp.arange(vocab_count)[None, None, :]).astype(jnp.int32)
    running = jnp.cumsum(onehot, axis=1)
    slot_rank = jnp.sum(onehot * running, axis=2) - 1
    return (owner_of, local_block, slot_rank)


def gather_rows(x, axis):
    count = lax.axis_size(axis)
    copies = jnp.broadcast_to(x[None], (count,) + x.shape).reshape((count * x.shape[0],) + x.shape[1:])
    return lax.all_to_all(copies, axis, split_axis=0, concat_axis=0, tiled=True)


def scatter_hidden(partial):
    dp = lax.axis_size("dp")
    vocab = lax.axis_size("vocab")
    core = lax.axis_index("dp") % 2
    tokens, features = partial.shape[0] // dp, partial.shape[1]
    parts = partial.astype(jnp.bfloat16).reshape(dp // 2, 2, tokens, features)
    kept = lax.dynamic_index_in_dim(parts, core, 1, keepdims=False)
    sent = lax.dynamic_index_in_dim(parts, 1 - core, 1, keepdims=False)
    got = lax.ppermute(sent, "dp", [(i, i ^ 1) for i in range(dp)])
    both = (kept.astype(jnp.float32) + got.astype(jnp.float32)).astype(jnp.bfloat16)
    groups = [[i for i in range(dp) if i % 2 == c] for c in range(2)]
    rows = lax.all_to_all(both, "dp", split_axis=0, concat_axis=0, axis_index_groups=groups, tiled=True)
    rows = jnp.sum(rows.astype(jnp.float32), axis=0).astype(jnp.bfloat16)
    last = rows.reshape(tokens, vocab, features // vocab).transpose(1, 0, 2)
    last = lax.all_to_all(last, "vocab", split_axis=0, concat_axis=0, tiled=True)
    return jnp.sum(last.astype(jnp.float32), axis=0).astype(jnp.bfloat16)


def body(student_hidden, head_weight, teacher_logprobs, align_index, align_tiles, grad_scale):
    vocab_count = lax.axis_size("vocab")
    dp_count = lax.axis_size("dp")
    own_index = lax.axis_index("vocab")
    dp_index = lax.axis_index("dp")
    tokens_here = student_hidden.shape[0]
    student_cols = head_weight.shape[1]
    student_count = student_cols // BLOCK
    teacher_count = teacher_logprobs.shape[1] // BLOCK
    pair_count = student_count * K
    capacity = (2 * pair_count + vocab_count - 1) // vocab_count
    all_rows = align_index.reshape(vocab_count, pair_count)
    owner_all, local_all, rank_all = pair_tables(all_rows, teacher_count, vocab_count)
    held_here = owner_all == own_index
    slot_numbers = jnp.arange(capacity)
    selected = (
        held_here[:, None, :] & (rank_all[:, None, :] == slot_numbers[None, :, None])
    ).astype(jnp.int32)
    source_block = jnp.sum(selected * local_all[:, None, :], axis=2).reshape(-1)
    own_owner = lax.dynamic_index_in_dim(owner_all, own_index, 0, keepdims=False)
    own_rank = lax.dynamic_index_in_dim(rank_all, own_index, 0, keepdims=False)
    where_from = own_owner * capacity + own_rank

    teacher_probs = (
        jnp.exp(teacher_logprobs).astype(jnp.bfloat16).reshape(tokens_here, teacher_count, BLOCK)
    ).transpose(1, 0, 2)
    outgoing = jnp.take(teacher_probs, source_block, axis=0)
    arrived = lax.all_to_all(outgoing, "vocab", split_axis=0, concat_axis=0, tiled=True)

    weight = lax.all_to_all(head_weight, "dp", split_axis=1, concat_axis=0, tiled=True)
    hidden = gather_rows(student_hidden, "dp")
    logits = jnp.dot(hidden, weight, preferred_element_type=jnp.float32)
    row_max = lax.pmax(jnp.max(logits, axis=1), ("dp", "vocab"))
    shifted = jnp.exp(logits - row_max[:, None])

    picked = jnp.take(arrived, where_from, axis=0).reshape(student_count, K, tokens_here, BLOCK)
    mapped_rows = jnp.einsum("bktj,bkji->tbi", picked, align_tiles, preferred_element_type=jnp.float32)
    mapped_rows = mapped_rows.reshape(tokens_here, student_cols)
    mapped = lax.all_to_all(
        mapped_rows.astype(jnp.bfloat16), "dp", split_axis=1, concat_axis=0, tiled=True
    )
    own_rows = (jnp.arange(dp_count) == dp_index).astype(jnp.float32)[:, None]
    first = (own_index == 0).astype(jnp.float32)
    mass_part = (own_rows * jnp.sum(mapped_rows, axis=1)[None]).reshape(-1)
    scale_part = (own_rows * (first * grad_scale)[None]).reshape(-1)
    row_total, mass, scale = lax.psum((jnp.sum(shifted, axis=1), mass_part, scale_part), ("dp", "vocab"))
    student_probs = shifted / row_total[:, None]
    dlogits = (
        scale[:, None] * (mass[:, None] * student_probs - mapped.astype(jnp.float32))
    ).astype(jnp.bfloat16)
    hidden_terms = lax.dot_general(
        dlogits, weight, (((1,), (1,)), ((), ())), preferred_element_type=jnp.float32
    )
    hidden_grad = scatter_hidden(hidden_terms)
    head_terms = lax.dot_general(
        hidden, dlogits, (((0,), (0,)), ((), ())), preferred_element_type=jnp.float32
    ).astype(jnp.bfloat16)
    head_grad = lax.all_to_all(head_terms, "dp", split_axis=0, concat_axis=1, tiled=True)
    return (hidden_grad, head_grad)


def solution(mesh):
    placed = (
        P("dp", None),
        P("dp", "vocab"),
        P("dp", "vocab"),
        P(),
        P("vocab", None, None, None),
        P("dp"),
    )
    return jax.shard_map(
        body,
        mesh=mesh,
        in_specs=placed,
        out_specs=(P("dp", "vocab"), P("dp", "vocab")),
        check_vma=False,
    )
```

```python
import functools

import jax
import jax.numpy as jnp
from jax import lax
from jax.experimental import pallas as pl
from jax.experimental.pallas import tpu as pltpu
from jax.sharding import PartitionSpec as P

BLOCK = 128
K = 2
CHUNKS = 2

ANY = pl.BlockSpec(memory_space=pl.ANY)
VMEM = pl.BlockSpec(memory_space=pltpu.VMEM)
F32 = jnp.float32
BF16 = jnp.bfloat16


def swap(x, axis, bits):
    return lax.ppermute(x, axis, [(i, i ^ bits) for i in range(lax.axis_size(axis))])


def probs_kernel(x_ref, *out_refs):
    rows = out_refs[0].shape[1]
    for j in range(out_refs[0].shape[0]):
        block = jnp.exp(x_ref[:, j * BLOCK : (j + 1) * BLOCK]).astype(BF16)
        for c, out in enumerate(out_refs):
            out[j] = block[c * rows : (c + 1) * rows]


def teacher_blocks(logprobs):
    tokens, cols = logprobs.shape
    count = cols // BLOCK
    step = next(s for s in (8, 5, 4, 2, 1) if count % s == 0)
    rows = tokens // CHUNKS
    return pl.pallas_call(
        probs_kernel,
        grid=(count // step,),
        in_specs=[pl.BlockSpec((tokens, step * BLOCK), lambda i: (0, i))],
        out_specs=[pl.BlockSpec((step, rows, BLOCK), lambda i: (i, 0, 0))] * CHUNKS,
        out_shape=[jax.ShapeDtypeStruct((count, rows, BLOCK), BF16)] * CHUNKS,
        name="probs",
    )(logprobs)


def pack_kernel(first, depth, vocab, tab_ref, own_ref, *refs):
    ups, downs, out_ref, sems = refs[:depth], refs[depth : 2 * depth], refs[2 * depth], refs[2 * depth + 1]
    me = tab_ref[8, 0]
    capacity = out_ref.shape[0]
    pairs = tab_ref.shape[1]
    for role, (node, rest) in enumerate(((1, downs), (vocab - 2, ups))):

        @pl.when(me == node)
        def _(role=role, rest=rest):
            def visit(p, started):
                slot = tab_ref[2 + role, p] - first

                @pl.when((slot >= 0) & (slot < capacity))
                def _():
                    if started:
                        pltpu.make_async_copy(own_ref.at[0], out_ref.at[0], sems.at[p]).wait()
                    else:
                        for d, source in enumerate((own_ref,) + rest):

                            @pl.when(tab_ref[4 + role, p] == d + 1)
                            def _(source=source):
                                pltpu.make_async_copy(
                                    source.at[tab_ref[6 + role, p]], out_ref.at[slot], sems.at[p]
                                ).start()

            lax.fori_loop(0, pairs, lambda p, c: (visit(p, False), c)[1], 0)
            lax.fori_loop(0, pairs, lambda p, c: (visit(p, True), c)[1], 0)


def pack(tab, first, capacity, own, ups, downs, vocab):
    return pl.pallas_call(
        functools.partial(pack_kernel, first, len(ups), vocab),
        grid_spec=pltpu.PrefetchScalarGridSpec(
            num_scalar_prefetch=1,
            grid=(),
            in_specs=[ANY] * (1 + 2 * len(ups)),
            out_specs=ANY,
            scratch_shapes=[pltpu.SemaphoreType.DMA((tab.shape[1],))],
        ),
        out_shape=jax.ShapeDtypeStruct((capacity,) + own.shape[1:], BF16),
        name="pack",
    )(tab, own, *ups, *downs)


def mapped_kernel(members, tab_ref, *refs):
    sources, tiles_ref, outs, buf, sems = refs[: -members - 3], refs[-members - 3], refs[-members - 2 : -2], refs[-2], refs[-1]
    me = tab_ref[8, 1]
    pairs = tab_ref.shape[1]
    per = outs[0].shape[1] // BLOCK

    def start(p, carry):
        for i, source in enumerate(sources):

            @pl.when(tab_ref[0, p] == i)
            def _(source=source):
                pltpu.make_async_copy(source.at[tab_ref[1, p]], buf.at[p], sems.at[p]).start()

        return carry

    def finish(p, carry):
        pltpu.make_async_copy(sources[0].at[0], buf.at[p], sems.at[p]).wait()
        return carry

    lax.fori_loop(0, pairs, start, 0)
    lax.fori_loop(0, pairs, finish, 0)
    for s, out in enumerate(outs):
        dest = lax.bitwise_xor(me, s)
        for j in range(per):
            b = dest * per + j
            total = jnp.dot(buf[K * b], tiles_ref[b, 0], preferred_element_type=F32)
            for k in range(1, K):
                total += jnp.dot(buf[K * b + k], tiles_ref[b, k], preferred_element_type=F32)
            out[:, j * BLOCK : (j + 1) * BLOCK] = total.astype(BF16)


def mapped_parts(tab, sources, tiles, members):
    rows = sources[0].shape[1]
    cols = tiles.shape[0] * BLOCK // members
    pairs = tab.shape[1]
    return pl.pallas_call(
        functools.partial(mapped_kernel, members),
        grid_spec=pltpu.PrefetchScalarGridSpec(
            num_scalar_prefetch=1,
            grid=(),
            in_specs=[ANY] * len(sources) + [VMEM],
            out_specs=[VMEM] * members,
            scratch_shapes=[pltpu.VMEM((pairs, rows, BLOCK), BF16), pltpu.SemaphoreType.DMA((pairs,))],
        ),
        out_shape=[jax.ShapeDtypeStruct((rows, cols), BF16)] * members,
        name="mapped",
    )(tab, *sources, tiles)


def logits_kernel(x_ref, w_ref, e_ref, m_ref, s_ref):
    logits = jnp.dot(x_ref[0], w_ref[...], preferred_element_type=F32)
    top = jnp.max(logits, axis=1, keepdims=True)
    e = jnp.exp(logits - top)
    e_ref[0] = e
    m_ref[0] = top
    s_ref[0] = jnp.sum(e, axis=1, keepdims=True)


def logits_parts(hidden, weight):
    members, tokens, features = hidden.shape
    cols = weight.shape[1]
    spec = lambda n: pl.BlockSpec((1, tokens, n), lambda i: (i, 0, 0))
    shape = lambda n: jax.ShapeDtypeStruct((members, tokens, n), F32)
    return pl.pallas_call(
        logits_kernel,
        grid=(members,),
        in_specs=[spec(features), pl.BlockSpec((features, cols), lambda i: (0, 0))],
        out_specs=[spec(cols), spec(1), spec(1)],
        out_shape=[shape(cols), shape(1), shape(1)],
        name="logits",
    )(hidden, weight)


def stats_kernel(order, top_ref, *refs):
    shares, out_ref = refs[:-1], refs[-1]
    members = len(order)
    for k, s in enumerate(order):
        rows = [order.index(s ^ r) for r in range(members)]
        tops = [shares[r][j : j + 1] for r, j in enumerate(rows)]
        top = functools.reduce(jnp.maximum, tops)
        total = sum(
            shares[r][members + j : members + j + 1] * jnp.exp(tops[r] - top) for r, j in enumerate(rows)
        )
        mass = shares[s][2 * members : 2 * members + 1]
        scale = shares[s][2 * members + 1 : 2 * members + 2]
        out_ref[0, k : k + 1] = scale * mass * (jnp.exp(top_ref[k : k + 1] - top) / total)
        out_ref[1, k : k + 1] = scale


def grads_kernel(members, e_ref, a_ref, b_ref, w_ref, *refs):
    mapped, dl_ref, kept_ref, sent_ref = refs[:members], refs[-3], refs[-2], refs[-1]
    half = members // 2
    for k in range(members):
        dl = (a_ref[k] * e_ref[k] - b_ref[k] * mapped[k][...].astype(F32)).astype(BF16)
        dl_ref[k] = dl
        terms = lax.dot_general(dl, w_ref[...], (((1,), (1,)), ((), ())), preferred_element_type=F32)
        if k < half:
            kept_ref[k] = terms.astype(BF16)
        else:
            sent_ref[k - half] = terms.astype(BF16)


def grads(chunk, e, a, b, weight, mapped):
    members, tokens, cols = e.shape
    features = weight.shape[0]
    rows = tokens // CHUNKS
    part = lambda n: pl.BlockSpec((members, rows, n), lambda i: (0, chunk, 0))
    whole = lambda *shape: pl.BlockSpec(shape, lambda i: (0,) * len(shape))
    halves = (members // 2, rows, features)
    return pl.pallas_call(
        functools.partial(grads_kernel, members),
        grid=(1,),
        in_specs=[part(cols), part(1), part(1), whole(features, cols)] + [whole(rows, cols)] * members,
        out_specs=[whole(members, rows, cols), whole(*halves), whole(*halves)],
        out_shape=[
            jax.ShapeDtypeStruct((members, rows, cols), BF16),
            jax.ShapeDtypeStruct(halves, BF16),
            jax.ShapeDtypeStruct(halves, BF16),
        ],
        name="grads",
    )(e, a, b, weight, *mapped)


def body(student_hidden, head_weight, teacher_logprobs, align_index, align_tiles, grad_scale):
    vocab = lax.axis_size("vocab")
    dp = lax.axis_size("dp")
    v = lax.axis_index("vocab")
    d = lax.axis_index("dp")
    tokens = student_hidden.shape[0]
    cols = head_weight.shape[1]
    count = teacher_logprobs.shape[1] // BLOCK
    pairs = align_tiles.shape[0] * K
    capacity = (2 * pairs + vocab - 1) // vocab
    packs = (pairs + capacity - 1) // capacity
    order = list(range(0, dp, 2)) + list(range(1, dp, 2))
    if vocab < 4 or vocab & (vocab - 1) or dp & (dp - 1):
        raise ValueError("mesh sizes")

    weight = lax.all_to_all(head_weight, "dp", split_axis=1, concat_axis=0, tiled=True)
    blocks = teacher_blocks(teacher_logprobs)

    rows = align_index.reshape(vocab, pairs)
    ends = jnp.stack([rows[0], rows[vocab - 1]])
    end_owner, end_local = lax.div(ends, jnp.int32(count)), lax.rem(ends, jnp.int32(count))
    end_far = jnp.abs(end_owner - jnp.array([[0], [vocab - 1]]))
    number = jnp.arange(pairs)
    later = (end_far[:, None, :] > end_far[:, :, None]) | (
        (end_far[:, None, :] == end_far[:, :, None]) & (number[None, None, :] >= number[None, :, None])
    )
    end_slot = packs * capacity - jnp.sum((later & (end_far[:, None, :] > 0)).astype(jnp.int32), axis=2)
    end_slot = jnp.where(end_far > 0, end_slot, -1)
    own = lax.dynamic_index_in_dim(rows, v, 0, keepdims=False)
    own_owner, own_local = lax.div(own, jnp.int32(count)), lax.rem(own, jnp.int32(count))
    own_slot = jnp.where(v == 0, end_slot[0], end_slot[1])
    at_end = ((v == 0) | (v == vocab - 1)) & (own_owner != v)
    source = jnp.where(own_owner <= v, v - own_owner, vocab - 2 + own_owner - v)
    source = jnp.where(at_end, 2 * vocab - 3 + lax.div(own_slot, jnp.int32(capacity)), source)
    place = jnp.where(at_end, lax.rem(own_slot, jnp.int32(capacity)), own_local)
    me = jnp.where(number == 0, v, d)
    tab = jnp.concatenate(
        [source[None], place[None], end_slot, end_far, end_local, me[None]], axis=0
    ).astype(jnp.int32)

    def exchange(own, after):
        if after is not None:
            own, _ = lax.optimization_barrier((own, after))
        ups, downs, packed = [], [], []
        up, down = own, own
        for r in range(1, vocab - 1):
            up = lax.ppermute(up, "vocab", [(i, i + 1) for i in range(r - 1, vocab - 2)])
            down = lax.ppermute(down, "vocab", [(i, i - 1) for i in range(2, vocab - r + 1)])
            ups.append(up)
            downs.append(down)
        for q in range(packs):
            depth = q + 1 - packs + vocab - 2
            part = pack(tab, q * capacity, capacity, own, ups[:depth], downs[:depth], vocab)
            packed.append(lax.ppermute(part, "vocab", [(vocab - 2, vocab - 1), (1, 0)]))
        return [own] + ups + downs + packed

    sources = []
    for c in range(CHUNKS):
        sources.append(exchange(blocks[c], sources[-1][1] if c else None))

    row_sums = jnp.sum(align_tiles.astype(F32), axis=3).reshape(pairs, BLOCK)
    all_sums = [row_sums] + [swap(row_sums, "vocab", t) for t in range(1, vocab)]
    all_rows = [own] + [lax.dynamic_index_in_dim(rows, v ^ t, 0, keepdims=False) for t in range(1, vocab)]
    hits = (jnp.concatenate(all_rows)[None, :] == (v * count + jnp.arange(count))[:, None]).astype(F32)
    entry_weight = jnp.dot(hits, jnp.concatenate(all_sums), precision=lax.Precision.HIGHEST)
    mass = jnp.concatenate(
        [jnp.sum(part.astype(F32) * entry_weight[:, None, :], axis=(0, 2)) for part in blocks]
    )

    even = jnp.stack([student_hidden] + [swap(student_hidden, "dp", s) for s in range(2, dp, 2)])
    hidden = jnp.concatenate([even, swap(even, "dp", 1)])
    e, top, total = logits_parts(hidden, weight)
    top, total = top.reshape(dp, tokens), total.reshape(dp, tokens)

    zeros = jnp.zeros((1, tokens), F32)
    share = jnp.concatenate([top, total, mass[None], zeros])
    shares = [share] + [swap(share, "vocab", t) for t in range(1, vocab)]
    plane_top = functools.reduce(jnp.maximum, [s[:dp] for s in shares])
    plane_total = sum(s[dp : 2 * dp] * jnp.exp(s[:dp] - plane_top) for s in shares)
    plane_mass = sum(s[2 * dp] for s in shares)
    share = jnp.concatenate([plane_top, plane_total, plane_mass[None], grad_scale[None]])
    shares = [share] + [swap(share, "dp", s) for s in range(1, dp)]
    coefs = pl.pallas_call(
        functools.partial(stats_kernel, order),
        in_specs=[VMEM] * (dp + 1),
        out_specs=VMEM,
        out_shape=jax.ShapeDtypeStruct((2, dp, tokens), F32),
        name="stats",
    )(top, *shares)
    a, b = coefs[0][..., None], coefs[1][..., None]

    dls, hiddens = [], []
    for c in range(CHUNKS):
        parts = mapped_parts(tab, sources[c], align_tiles, dp)
        parts = [parts[s] if s == 0 else swap(parts[s], "dp", s) for s in order]
        dl, kept, sent = grads(c, e, a, b, weight, parts)
        dls.append(dl)
        both = (kept.astype(F32) + swap(sent, "dp", 1).astype(F32)).astype(BF16)
        rows_sum = both[0].astype(F32)
        for j in range(1, dp // 2):
            rows_sum += swap(both[j], "dp", 2 * j).astype(F32)
        rows_sum = rows_sum.astype(BF16)
        width = rows_sum.shape[1] // vocab
        piece = lambda t: lax.dynamic_slice_in_dim(rows_sum, (v ^ t) * width, width, 1)
        out = piece(0).astype(F32)
        for t in range(1, vocab):
            out += swap(piece(t), "vocab", t).astype(F32)
        hiddens.append(out.astype(BF16))
    dl = jnp.concatenate(dls, axis=1)
    head_terms = lax.dot_general(
        hidden.reshape(dp * tokens, -1),
        dl.reshape(dp * tokens, -1),
        (((0,), (0,)), ((), ())),
        preferred_element_type=F32,
    ).astype(BF16)
    head_grad = lax.all_to_all(head_terms, "dp", split_axis=0, concat_axis=1, tiled=True)
    return (jnp.concatenate(hiddens), head_grad)


def solution(mesh):
    placed = (
        P("dp", None),
        P("dp", "vocab"),
        P("dp", "vocab"),
        P(),
        P("vocab", None, None, None),
        P("dp"),
    )
    return jax.shard_map(
        body,
        mesh=mesh,
        in_specs=placed,
        out_specs=(P("dp", "vocab"), P("dp", "vocab")),
        check_vma=False,
    )
```

```python
import functools

import jax
import jax.numpy as jnp
from jax import lax
from jax.experimental import pallas as pl
from jax.experimental.pallas import tpu as pltpu
from jax.sharding import PartitionSpec as P

BLOCK = 128
K = 2
CHUNKS = 2

ANY = pl.BlockSpec(memory_space=pl.ANY)
VMEM = pl.BlockSpec(memory_space=pltpu.VMEM)
F32 = jnp.float32
BF16 = jnp.bfloat16


def swap(x, axis, bits):
    return lax.ppermute(x, axis, [(i, i ^ bits) for i in range(lax.axis_size(axis))])


def probs_kernel(x_ref, *out_refs):
    rows = out_refs[0].shape[1]
    for j in range(out_refs[0].shape[0]):
        block = jnp.exp(x_ref[:, j * BLOCK : (j + 1) * BLOCK]).astype(BF16)
        for c, out in enumerate(out_refs):
            out[j] = block[c * rows : (c + 1) * rows]


def teacher_blocks(logprobs):
    tokens, cols = logprobs.shape
    count = cols // BLOCK
    step = next(s for s in (8, 5, 4, 2, 1) if count % s == 0)
    rows = tokens // CHUNKS
    return pl.pallas_call(
        probs_kernel,
        grid=(count // step,),
        in_specs=[pl.BlockSpec((tokens, step * BLOCK), lambda i: (0, i))],
        out_specs=[pl.BlockSpec((step, rows, BLOCK), lambda i: (i, 0, 0))] * CHUNKS,
        out_shape=[jax.ShapeDtypeStruct((count, rows, BLOCK), BF16)] * CHUNKS,
        name="probs",
    )(logprobs)


def pack_kernel(first, vocab, tab_ref, *refs):
    sources, out_ref, sems = refs[:-2], refs[-2], refs[-1]
    v = tab_ref[8, 0]
    capacity = out_ref.shape[0]
    row = jnp.where(v == 1, 0, 1)

    def visit(p, started):
        slot = tab_ref[2 + row, p] - first

        @pl.when((slot >= 0) & (slot < capacity))
        def _():
            if started:
                pltpu.make_async_copy(sources[0].at[0], out_ref.at[0], sems.at[p]).wait()
            else:
                for d, source in enumerate(sources):

                    @pl.when(tab_ref[4 + row, p] == d + 1)
                    def _(source=source):
                        pltpu.make_async_copy(
                            source.at[tab_ref[6 + row, p]], out_ref.at[slot], sems.at[p]
                        ).start()

    @pl.when((v == 1) | (v == vocab - 2))
    def _():
        for started in (False, True):
            lax.fori_loop(0, tab_ref.shape[1], lambda p, c: (visit(p, started), c)[1], 0)


def pack(tab, first, capacity, sources, vocab):
    return pl.pallas_call(
        functools.partial(pack_kernel, first, vocab),
        grid_spec=pltpu.PrefetchScalarGridSpec(
            num_scalar_prefetch=1,
            grid=(),
            in_specs=[ANY] * len(sources),
            out_specs=ANY,
            scratch_shapes=[pltpu.SemaphoreType.DMA((tab.shape[1],))],
        ),
        out_shape=jax.ShapeDtypeStruct((capacity,) + sources[0].shape[1:], BF16),
        name="pack",
    )(tab, *sources)


def mapped_kernel(chips, tab_ref, *refs):
    count = (len(refs) - 3 - chips) // CHUNKS
    chunks = [refs[c * count : (c + 1) * count] for c in range(CHUNKS)]
    tiles_ref, outs, buf, sems = refs[CHUNKS * count], refs[CHUNKS * count + 1 : -2], refs[-2], refs[-1]
    me = tab_ref[8, 1]
    pairs = tab_ref.shape[1]
    rows = chunks[0][0].shape[1]
    per = outs[0].shape[1] // BLOCK

    def start(p, carry):
        for c, sources in enumerate(chunks):
            for i, source in enumerate(sources):

                @pl.when(tab_ref[0, p] == i)
                def _(c=c, source=source):
                    pltpu.make_async_copy(
                        source.at[tab_ref[1, p]], buf.at[p, pl.ds(c * rows, rows)], sems.at[c, p]
                    ).start()

        return carry

    def finish(p, carry):
        for c, sources in enumerate(chunks):
            pltpu.make_async_copy(sources[0].at[0], buf.at[p, pl.ds(c * rows, rows)], sems.at[c, p]).wait()
        return carry

    lax.fori_loop(0, pairs, start, 0)
    lax.fori_loop(0, pairs, finish, 0)
    for s, out in enumerate(outs):
        dest = lax.bitwise_xor(me, s)
        for j in range(per):
            b = dest * per + j
            total = jnp.dot(buf[K * b], tiles_ref[b, 0], preferred_element_type=F32)
            for k in range(1, K):
                total += jnp.dot(buf[K * b + k], tiles_ref[b, k], preferred_element_type=F32)
            out[:, j * BLOCK : (j + 1) * BLOCK] = total.astype(BF16)


def mapped_parts(tab, sources, tiles, chips):
    tokens = CHUNKS * sources[0][0].shape[1]
    cols = tiles.shape[0] * BLOCK // chips
    pairs = tab.shape[1]
    flat = [x for part in sources for x in part]
    return pl.pallas_call(
        functools.partial(mapped_kernel, chips),
        grid_spec=pltpu.PrefetchScalarGridSpec(
            num_scalar_prefetch=1,
            grid=(),
            in_specs=[ANY] * len(flat) + [VMEM],
            out_specs=[VMEM] * chips,
            scratch_shapes=[
                pltpu.VMEM((pairs, tokens, BLOCK), BF16),
                pltpu.SemaphoreType.DMA((CHUNKS, pairs)),
            ],
        ),
        out_shape=[jax.ShapeDtypeStruct((tokens, cols), BF16)] * chips,
        name="mapped",
    )(tab, *flat, tiles)


def logits_kernel(core_ref, x_ref, own_ref, other_ref, e_ref, m_ref, s_ref):
    c = core_ref[0]
    logits = jnp.dot(x_ref[c], own_ref[...], preferred_element_type=F32)
    logits += jnp.dot(x_ref[1 - c], other_ref[...], preferred_element_type=F32)
    top = jnp.max(logits, axis=1, keepdims=True)
    e = jnp.exp(logits - top)
    e_ref[...] = e
    m_ref[...] = top
    s_ref[...] = jnp.sum(e, axis=1, keepdims=True)


def logits_parts(core, hidden, own, other, tokens):
    rows = hidden.shape[1]
    features, cols = own.shape
    spec = lambda n: pl.BlockSpec((tokens, n), lambda i, core: (i, 0))
    shape = lambda n: jax.ShapeDtypeStruct((rows, n), F32)
    fixed = pl.BlockSpec((features, cols), lambda i, core: (0, 0))
    return pl.pallas_call(
        logits_kernel,
        grid_spec=pltpu.PrefetchScalarGridSpec(
            num_scalar_prefetch=1,
            grid=(rows // tokens,),
            in_specs=[pl.BlockSpec((2, tokens, features), lambda i, core: (0, i, 0)), fixed, fixed],
            out_specs=[spec(cols), spec(1), spec(1)],
        ),
        out_shape=[shape(cols), shape(1), shape(1)],
        name="logits",
    )(core, hidden, own, other)


def stats_kernel(top_ref, *refs):
    shares, out_ref = refs[:-1], refs[-1]
    chips = len(shares)
    for k in range(chips):
        rows = [k ^ r for r in range(chips)]
        tops = [shares[r][j : j + 1] for r, j in enumerate(rows)]
        top = functools.reduce(jnp.maximum, tops)
        total = sum(shares[r][chips + j : chips + j + 1] * jnp.exp(tops[r] - top) for r, j in enumerate(rows))
        mass = shares[k][2 * chips : 2 * chips + 1]
        scale = shares[k][2 * chips + 1 : 2 * chips + 2]
        out_ref[0, k : k + 1] = scale * mass * (jnp.exp(top_ref[k : k + 1] - top) / total)
        out_ref[1, k : k + 1] = scale


def grads_kernel(chips, core_ref, e_ref, a_ref, b_ref, own_ref, other_ref, *refs):
    mapped, dl_ref, outs = refs[:chips], refs[chips], refs[chips + 1 :]
    c = core_ref[0]
    tokens = mapped[0].shape[0]
    for k in range(chips):
        rows = slice(k * tokens, (k + 1) * tokens)
        dl = (a_ref[rows] * e_ref[rows] - b_ref[rows] * mapped[k][...].astype(F32)).astype(BF16)
        dl_ref[rows] = dl
        for half, weight in ((c, own_ref), (1 - c, other_ref)):
            terms = lax.dot_general(dl, weight[...], (((1,), (1,)), ((), ())), preferred_element_type=F32)
            outs[k][half] = terms.astype(BF16)


def grads(core, e, a, b, own, other, mapped):
    chips, tokens = len(mapped), mapped[0].shape[0]
    return pl.pallas_call(
        functools.partial(grads_kernel, chips),
        grid_spec=pltpu.PrefetchScalarGridSpec(
            num_scalar_prefetch=1,
            grid=(),
            in_specs=[VMEM] * (5 + chips),
            out_specs=[VMEM] * (1 + chips),
        ),
        out_shape=[jax.ShapeDtypeStruct(e.shape, BF16)]
        + [jax.ShapeDtypeStruct((2, tokens, own.shape[0]), BF16)] * chips,
        name="grads",
    )(core, e, a, b, own, other, *mapped)


def body(student_hidden, head_weight, teacher_logprobs, align_index, align_tiles, grad_scale):
    vocab = lax.axis_size("vocab")
    dp = lax.axis_size("dp")
    v = lax.axis_index("vocab")
    d = lax.axis_index("dp")
    chips, chip, c = dp // 2, d // 2, d % 2
    core = c.astype(jnp.int32)[None]
    tokens, features = student_hidden.shape
    count = teacher_logprobs.shape[1] // BLOCK
    pairs = align_tiles.shape[0] * K
    capacity = (2 * pairs + vocab - 1) // vocab
    packs = (pairs + capacity - 1) // capacity
    if vocab < 4 or vocab & (vocab - 1) or dp & (dp - 1):
        raise ValueError("mesh sizes")
    groups = [[2 * i + j for i in range(chips)] for j in range(2)]

    blocks = teacher_blocks(teacher_logprobs)

    hops = [(r, i) for r in range(1, vocab - 1) for i in range(r - 1, vocab - 2)]
    number_of = [[0] * vocab for _ in range(vocab)]
    for i in range(1, vocab - 1):
        for o in range(vocab):
            if o != i:
                link = i - 1 if o < i else vocab - 2 - i
                number_of[i][o] = 1 + hops.index((abs(o - i), link))

    rows = align_index.reshape(vocab, pairs)
    ends = jnp.stack([rows[0], rows[vocab - 1]])
    end_owner, end_local = lax.div(ends, jnp.int32(count)), lax.rem(ends, jnp.int32(count))
    end_far = jnp.abs(end_owner - jnp.array([[0], [vocab - 1]]))
    number = jnp.arange(pairs)
    later = (end_far[:, None, :] > end_far[:, :, None]) | (
        (end_far[:, None, :] == end_far[:, :, None]) & (number[None, None, :] >= number[None, :, None])
    )
    end_slot = packs * capacity - jnp.sum((later & (end_far[:, None, :] > 0)).astype(jnp.int32), axis=2)
    end_slot = jnp.where(end_far > 0, end_slot, -1)
    own = lax.dynamic_index_in_dim(rows, v, 0, keepdims=False)
    own_owner, own_local = lax.div(own, jnp.int32(count)), lax.rem(own, jnp.int32(count))
    own_slot = jnp.where(v == 0, end_slot[0], end_slot[1])
    at_end = ((v == 0) | (v == vocab - 1)) & (own_owner != v)
    numbers = lax.dynamic_index_in_dim(jnp.array(number_of, jnp.int32), v, 0, keepdims=False)
    source = jnp.sum(
        jnp.where(own_owner[None, :] == jnp.arange(vocab)[:, None], numbers[:, None], 0), axis=0
    )
    source = jnp.where(at_end, 1 + len(hops) + lax.div(own_slot, jnp.int32(capacity)), source)
    place = jnp.where(at_end, lax.rem(own_slot, jnp.int32(capacity)), own_local)
    me = jnp.where(number == 0, v, chip)
    tab = jnp.concatenate(
        [source[None], place[None], end_slot, end_far, end_local, me[None]], axis=0
    ).astype(jnp.int32)

    def exchange(own_blocks, after):
        if after is not None:
            own_blocks, _ = lax.optimization_barrier((own_blocks, after))
        moved = {(0, i): own_blocks for i in range(-1, vocab)}
        for r, i in hops:
            moved[r, i] = lax.ppermute(
                moved[r - 1, i - 1], "vocab", [(i, i + 1), (vocab - 1 - i, vocab - 2 - i)]
            )
        near = [own_blocks] + [moved[r, vocab - 3] for r in range(1, vocab - 1)]
        packed = []
        for q in range(packs):
            part = pack(tab, q * capacity, capacity, near[: q - packs + vocab], vocab)
            packed.append(lax.ppermute(part, "vocab", [(vocab - 2, vocab - 1), (1, 0)]))
        return [own_blocks] + [moved[hop] for hop in hops] + packed

    sources = []
    for n in range(CHUNKS):
        sources.append(exchange(blocks[n], sources[-1][1] if n else None))

    weight_own = lax.all_to_all(
        head_weight, "dp", split_axis=1, concat_axis=0, axis_index_groups=groups, tiled=True
    )
    weight_other = swap(weight_own, "dp", 1)

    hidden = student_hidden.reshape(tokens, chips, 2, features // dp).transpose(2, 0, 1, 3)
    hidden = hidden.reshape(2, tokens, features // 2)
    hidden = jnp.concatenate([hidden] + [swap(hidden, "dp", 2 * j) for j in range(1, chips)], axis=1)
    e, top, total = logits_parts(core, hidden, weight_own, weight_other, tokens)
    top, total = top.reshape(chips, tokens), total.reshape(chips, tokens)

    row_sums = jnp.sum(align_tiles.astype(F32), axis=3).reshape(pairs, BLOCK)
    all_sums = [row_sums] + [swap(row_sums, "vocab", t) for t in range(1, vocab)]
    all_rows = [own] + [lax.dynamic_index_in_dim(rows, v ^ t, 0, keepdims=False) for t in range(1, vocab)]
    hits = (jnp.concatenate(all_rows)[None, :] == (v * count + jnp.arange(count))[:, None]).astype(F32)
    entry_weight = jnp.dot(hits, jnp.concatenate(all_sums), precision=lax.Precision.HIGHEST)
    mass = jnp.concatenate(
        [jnp.sum(part.astype(F32) * entry_weight[:, None, :], axis=(0, 2)) for part in blocks]
    )

    share = jnp.concatenate([top, total, mass[None]])
    shares = [share] + [swap(share, "vocab", t) for t in range(1, vocab)]
    plane_top = functools.reduce(jnp.maximum, [s[:chips] for s in shares])
    plane_total = sum(s[chips : 2 * chips] * jnp.exp(s[:chips] - plane_top) for s in shares)
    plane_mass = sum(s[2 * chips] for s in shares)
    share = jnp.concatenate([plane_top, plane_total, plane_mass[None], grad_scale[None]])
    shares = [share] + [swap(share, "dp", 2 * j) for j in range(1, chips)]
    coefs = pl.pallas_call(
        stats_kernel,
        in_specs=[VMEM] * (chips + 1),
        out_specs=VMEM,
        out_shape=jax.ShapeDtypeStruct((2, chips, tokens), F32),
        name="stats",
    )(top, *shares)
    a, b = coefs[0].reshape(-1, 1), coefs[1].reshape(-1, 1)

    parts = mapped_parts(tab, sources, align_tiles, chips)
    parts = [parts[0]] + [swap(parts[j], "dp", 2 * j) for j in range(1, chips)]
    dl, *terms = grads(core, e, a, b, weight_own, weight_other, parts)

    rows_sum = terms[0].astype(F32)
    for j in range(1, chips):
        rows_sum += swap(terms[j], "dp", 2 * j).astype(F32)
    rows_sum = rows_sum.astype(BF16).reshape(2, tokens, chips, features // dp).transpose(1, 2, 0, 3)
    pieces = rows_sum.reshape(tokens, vocab, features // vocab).transpose(1, 0, 2)
    piece = lambda t: lax.dynamic_index_in_dim(pieces, v ^ t, 0, keepdims=False)
    hidden_grad = piece(0).astype(F32)
    for t in range(1, vocab):
        hidden_grad += swap(piece(t), "vocab", t).astype(F32)

    def head_half(half):
        x = lax.dynamic_index_in_dim(hidden, half, 0, keepdims=False)
        return lax.dot_general(x, dl, (((0,), (0,)), ((), ())), preferred_element_type=F32).astype(BF16)

    got = swap(head_half(1 - c), "dp", 1)
    head_terms = (head_half(c).astype(F32) + got.astype(F32)).astype(BF16)
    head_grad = lax.all_to_all(
        head_terms, "dp", split_axis=0, concat_axis=1, axis_index_groups=groups, tiled=True
    )
    return (hidden_grad.astype(BF16), head_grad)


def solution(mesh):
    placed = (
        P("dp", None),
        P("dp", "vocab"),
        P("dp", "vocab"),
        P(),
        P("vocab", None, None, None),
        P("dp"),
    )
    return jax.shard_map(
        body,
        mesh=mesh,
        in_specs=placed,
        out_specs=(P("dp", "vocab"), P("dp", "vocab")),
        check_vma=False,
    )
```

```python
import functools

import jax
import jax.numpy as jnp
from jax import lax
from jax.experimental import pallas as pl
from jax.experimental.pallas import tpu as pltpu
from jax.sharding import PartitionSpec as P


BLOCK = 128
K = 2
CHUNKS = 2

ANY = pl.BlockSpec(memory_space=pl.ANY)
VMEM = pl.BlockSpec(memory_space=pltpu.VMEM)
F32 = jnp.float32
BF16 = jnp.bfloat16


def swap(x, axis, bits):
    return lax.ppermute(x, axis, [(i, i ^ bits) for i in range(lax.axis_size(axis))])


def probs_kernel(x_ref, *out_refs):
    rows = out_refs[0].shape[1]
    for j in range(out_refs[0].shape[0]):
        block = jnp.exp(x_ref[:, j * BLOCK : (j + 1) * BLOCK]).astype(BF16)
        for c, out in enumerate(out_refs):
            out[j] = block[c * rows : (c + 1) * rows]


def teacher_blocks(logprobs):
    tokens, cols = logprobs.shape
    count = cols // BLOCK
    step = next(s for s in (8, 5, 4, 2, 1) if count % s == 0)
    rows = tokens // CHUNKS
    return pl.pallas_call(
        probs_kernel,
        grid=(count // step,),
        in_specs=[pl.BlockSpec((tokens, step * BLOCK), lambda i: (0, i))],
        out_specs=[pl.BlockSpec((step, rows, BLOCK), lambda i: (i, 0, 0))] * CHUNKS,
        out_shape=[jax.ShapeDtypeStruct((count, rows, BLOCK), BF16)] * CHUNKS,
        name="probs",
    )(logprobs)


def pack_kernel(first, vocab, tab_ref, *refs):
    sources, out_ref, sems = refs[:-2], refs[-2], refs[-1]
    v = tab_ref[8, 0]
    capacity = out_ref.shape[0]
    row = jnp.where(v == 1, 0, 1)

    def visit(p, started):
        slot = tab_ref[2 + row, p] - first

        @pl.when((slot >= 0) & (slot < capacity))
        def _():
            if started:
                pltpu.make_async_copy(sources[0].at[0], out_ref.at[0], sems.at[p]).wait()
            else:
                for d, source in enumerate(sources):

                    @pl.when(tab_ref[4 + row, p] == d + 1)
                    def _(source=source):
                        pltpu.make_async_copy(
                            source.at[tab_ref[6 + row, p]], out_ref.at[slot], sems.at[p]
                        ).start()

    @pl.when((v == 1) | (v == vocab - 2))
    def _():
        for started in (False, True):
            lax.fori_loop(0, tab_ref.shape[1], lambda p, c: (visit(p, started), c)[1], 0)


def pack(tab, first, capacity, sources, vocab):
    return pl.pallas_call(
        functools.partial(pack_kernel, first, vocab),
        grid_spec=pltpu.PrefetchScalarGridSpec(
            num_scalar_prefetch=1,
            grid=(),
            in_specs=[ANY] * len(sources),
            out_specs=VMEM,
            scratch_shapes=[pltpu.SemaphoreType.DMA((tab.shape[1],))],
        ),
        out_shape=jax.ShapeDtypeStruct((capacity,) + sources[0].shape[1:], BF16),
        name="pack",
    )(tab, *sources)


def mapped_kernel(chips, tab_ref, *refs):
    sources, tiles_ref, outs, buf, sems = refs[: -chips - 3], refs[-chips - 3], refs[-chips - 2 : -2], refs[-2], refs[-1]
    me = tab_ref[8, 1]
    pairs = tab_ref.shape[1]
    per = outs[0].shape[1] // BLOCK

    def start(p, carry):
        for i, source in enumerate(sources):

            @pl.when(tab_ref[0, p] == i)
            def _(source=source):
                pltpu.make_async_copy(source.at[tab_ref[1, p]], buf.at[p], sems.at[p]).start()

        return carry

    def finish(p, carry):
        pltpu.make_async_copy(sources[0].at[0], buf.at[p], sems.at[p]).wait()
        return carry

    lax.fori_loop(0, pairs, start, 0)
    lax.fori_loop(0, pairs, finish, 0)
    for s, out in enumerate(outs):
        dest = lax.bitwise_xor(me, s)
        for j in range(per):
            b = dest * per + j
            total = jnp.dot(buf[K * b], tiles_ref[b, 0], preferred_element_type=F32)
            for k in range(1, K):
                total += jnp.dot(buf[K * b + k], tiles_ref[b, k], preferred_element_type=F32)
            out[:, j * BLOCK : (j + 1) * BLOCK] = total.astype(BF16)


def mapped_parts(tab, sources, tiles, chips):
    rows = sources[0].shape[1]
    cols = tiles.shape[0] * BLOCK // chips
    pairs = tab.shape[1]
    return pl.pallas_call(
        functools.partial(mapped_kernel, chips),
        grid_spec=pltpu.PrefetchScalarGridSpec(
            num_scalar_prefetch=1,
            grid=(),
            in_specs=[ANY] * len(sources) + [VMEM],
            out_specs=[VMEM] * chips,
            scratch_shapes=[pltpu.VMEM((pairs, rows, BLOCK), BF16), pltpu.SemaphoreType.DMA((pairs,))],
        ),
        out_shape=[jax.ShapeDtypeStruct((rows, cols), BF16)] * chips,
        name="mapped",
    )(tab, *sources, tiles)


def logits_kernel(core_ref, x_ref, own_ref, other_ref, e_ref, m_ref, s_ref):
    c = core_ref[0]
    logits = jnp.dot(x_ref[c], own_ref[...], preferred_element_type=F32)
    logits += jnp.dot(x_ref[1 - c], other_ref[...], preferred_element_type=F32)
    top = jnp.max(logits, axis=1, keepdims=True)
    e = jnp.exp(logits - top)
    e_ref[...] = e
    m_ref[...] = top
    s_ref[...] = jnp.sum(e, axis=1, keepdims=True)


def logits_parts(core, hidden, own, other, tokens):
    rows = hidden.shape[1]
    features, cols = own.shape
    spec = lambda n: pl.BlockSpec((tokens, n), lambda i, core: (i, 0))
    shape = lambda n: jax.ShapeDtypeStruct((rows, n), F32)
    fixed = pl.BlockSpec((features, cols), lambda i, core: (0, 0))
    return pl.pallas_call(
        logits_kernel,
        grid_spec=pltpu.PrefetchScalarGridSpec(
            num_scalar_prefetch=1,
            grid=(rows // tokens,),
            in_specs=[pl.BlockSpec((2, tokens, features), lambda i, core: (0, i, 0)), fixed, fixed],
            out_specs=[spec(cols), spec(1), spec(1)],
        ),
        out_shape=[shape(cols), shape(1), shape(1)],
        name="logits",
    )(core, hidden, own, other)


def stats_kernel(top_ref, *refs):
    shares, out_ref = refs[:-1], refs[-1]
    chips = len(shares)
    for k in range(chips):
        rows = [k ^ r for r in range(chips)]
        tops = [shares[r][j : j + 1] for r, j in enumerate(rows)]
        top = functools.reduce(jnp.maximum, tops)
        total = sum(shares[r][chips + j : chips + j + 1] * jnp.exp(tops[r] - top) for r, j in enumerate(rows))
        mass = shares[k][2 * chips : 2 * chips + 1]
        scale = shares[k][2 * chips + 1 : 2 * chips + 2]
        out_ref[0, k : k + 1] = scale * mass * (jnp.exp(top_ref[k : k + 1] - top) / total)
        out_ref[1, k : k + 1] = scale


def grads_kernel(chips, core_ref, e_ref, a_ref, b_ref, own_ref, other_ref, *refs):
    mapped, dl_ref, outs = refs[:chips], refs[-chips - 1], refs[-chips:]
    c = core_ref[0]
    for k in range(chips):
        dl = (a_ref[k] * e_ref[k] - b_ref[k] * mapped[k][...].astype(F32)).astype(BF16)
        dl_ref[k] = dl
        for half, weight in ((c, own_ref), (1 - c, other_ref)):
            terms = lax.dot_general(dl, weight[...], (((1,), (1,)), ((), ())), preferred_element_type=F32)
            outs[k][half] = terms.astype(BF16)


def grads(chunk, core, e, a, b, own, other, mapped, dl):
    chips, rows = len(mapped), mapped[0].shape[0]
    features, cols = own.shape
    part = lambda n: pl.BlockSpec((chips, rows, n), lambda i, core: (0, chunk, 0))
    whole = lambda *shape: pl.BlockSpec(shape, lambda i, core: (0,) * len(shape))
    return pl.pallas_call(
        functools.partial(grads_kernel, chips),
        grid_spec=pltpu.PrefetchScalarGridSpec(
            num_scalar_prefetch=1,
            grid=(1,),
            in_specs=[part(cols), part(1), part(1), whole(features, cols), whole(features, cols)]
            + [whole(rows, cols)] * chips
            + ([] if dl is None else [ANY]),
            out_specs=[part(cols)] + [whole(2, rows, features)] * chips,
        ),
        out_shape=[jax.ShapeDtypeStruct(e.shape, BF16)]
        + [jax.ShapeDtypeStruct((2, rows, features), BF16)] * chips,
        input_output_aliases={} if dl is None else {6 + chips: 0},
        name="grads",
    )(core, e, a, b, own, other, *mapped, *([] if dl is None else [dl]))


def body(student_hidden, head_weight, teacher_logprobs, align_index, align_tiles, grad_scale):
    vocab = lax.axis_size("vocab")
    dp = lax.axis_size("dp")
    v = lax.axis_index("vocab")
    d = lax.axis_index("dp")
    chips, chip, c = dp // 2, d // 2, d % 2
    core = c.astype(jnp.int32)[None]
    tokens, features = student_hidden.shape
    count = teacher_logprobs.shape[1] // BLOCK
    pairs = align_tiles.shape[0] * K
    capacity = (2 * pairs + vocab - 1) // vocab
    packs = (pairs + capacity - 1) // capacity
    if vocab < 4 or vocab & (vocab - 1) or dp & (dp - 1):
        raise ValueError("mesh sizes")
    groups = [[2 * i + j for i in range(chips)] for j in range(2)]

    blocks = teacher_blocks(teacher_logprobs)

    hops = [(r, i) for r in range(1, vocab - 1) for i in range(r - 1, vocab - 2)]
    number_of = [[0] * vocab for _ in range(vocab)]
    for i in range(1, vocab - 1):
        for o in range(vocab):
            if o != i:
                link = i - 1 if o < i else vocab - 2 - i
                number_of[i][o] = 1 + hops.index((abs(o - i), link))

    rows = align_index.reshape(vocab, pairs)
    ends = jnp.stack([rows[0], rows[vocab - 1]])
    end_owner, end_local = lax.div(ends, jnp.int32(count)), lax.rem(ends, jnp.int32(count))
    end_far = jnp.abs(end_owner - jnp.array([[0], [vocab - 1]]))
    number = jnp.arange(pairs)
    later = (end_far[:, None, :] > end_far[:, :, None]) | (
        (end_far[:, None, :] == end_far[:, :, None]) & (number[None, None, :] >= number[None, :, None])
    )
    end_slot = packs * capacity - jnp.sum((later & (end_far[:, None, :] > 0)).astype(jnp.int32), axis=2)
    end_slot = jnp.where(end_far > 0, end_slot, -1)
    own = lax.dynamic_index_in_dim(rows, v, 0, keepdims=False)
    own_owner, own_local = lax.div(own, jnp.int32(count)), lax.rem(own, jnp.int32(count))
    own_slot = jnp.where(v == 0, end_slot[0], end_slot[1])
    at_end = ((v == 0) | (v == vocab - 1)) & (own_owner != v)
    numbers = lax.dynamic_index_in_dim(jnp.array(number_of, jnp.int32), v, 0, keepdims=False)
    source = jnp.sum(
        jnp.where(own_owner[None, :] == jnp.arange(vocab)[:, None], numbers[:, None], 0), axis=0
    )
    source = jnp.where(at_end, 1 + len(hops) + lax.div(own_slot, jnp.int32(capacity)), source)
    place = jnp.where(at_end, lax.rem(own_slot, jnp.int32(capacity)), own_local)
    me = jnp.where(number == 0, v, chip)
    tab = jnp.concatenate(
        [source[None], place[None], end_slot, end_far, end_local, me[None]], axis=0
    ).astype(jnp.int32)

    def exchange(own_blocks):
        moved = {(0, i): own_blocks for i in range(-1, vocab)}
        for r, i in hops:
            moved[r, i] = lax.ppermute(
                moved[r - 1, i - 1], "vocab", [(i, i + 1), (vocab - 1 - i, vocab - 2 - i)]
            )
        near = [own_blocks] + [moved[r, vocab - 3] for r in range(1, vocab - 1)]
        packed = []
        for q in range(packs):
            part = pack(tab, q * capacity, capacity, near[: q - packs + vocab], vocab)
            packed.append(lax.ppermute(part, "vocab", [(vocab - 2, vocab - 1), (1, 0)]))
        return [own_blocks] + [moved[hop] for hop in hops] + packed

    sources = [exchange(part) for part in blocks]

    weight_own = lax.all_to_all(head_weight, "dp", split_axis=1, concat_axis=0, axis_index_groups=groups, tiled=True)
    weight_other = swap(weight_own, "dp", 1)

    hidden = student_hidden.reshape(tokens, chips, 2, features // dp).transpose(2, 0, 1, 3)
    hidden = hidden.reshape(2, tokens, features // 2)
    others = [swap(hidden, "dp", 2 * j) for j in range(1, chips)]
    hidden = jnp.concatenate([hidden] + others, axis=1)
    e, top, total = logits_parts(core, hidden, weight_own, weight_other, tokens)
    top, total = top.reshape(chips, tokens), total.reshape(chips, tokens)

    row_sums = jnp.sum(align_tiles.astype(F32), axis=3).reshape(pairs, BLOCK)
    all_sums = [row_sums] + [swap(row_sums, "vocab", t) for t in range(1, vocab)]
    all_rows = [own] + [lax.dynamic_index_in_dim(rows, v ^ t, 0, keepdims=False) for t in range(1, vocab)]
    hits = (jnp.concatenate(all_rows)[None, :] == (v * count + jnp.arange(count))[:, None]).astype(F32)
    entry_weight = jnp.dot(hits, jnp.concatenate(all_sums), precision=lax.Precision.HIGHEST)
    mass = jnp.concatenate(
        [jnp.sum(part.astype(F32) * entry_weight[:, None, :], axis=(0, 2)) for part in blocks]
    )

    share = jnp.concatenate([top, total, mass[None]])
    shares = [share] + [swap(share, "vocab", t) for t in range(1, vocab)]
    plane_top = functools.reduce(jnp.maximum, [s[:chips] for s in shares])
    plane_total = sum(s[chips : 2 * chips] * jnp.exp(s[:chips] - plane_top) for s in shares)
    plane_mass = sum(s[2 * chips] for s in shares)
    share = jnp.concatenate([plane_top, plane_total, plane_mass[None], grad_scale[None]])
    shares = [share] + [swap(share, "dp", 2 * j) for j in range(1, chips)]
    coefs = pl.pallas_call(
        stats_kernel,
        in_specs=[VMEM] * (chips + 1),
        out_specs=VMEM,
        out_shape=jax.ShapeDtypeStruct((2, chips, tokens), F32),
        name="stats",
    )(top, *shares)
    a, b = coefs[0][..., None], coefs[1][..., None]
    e = e.reshape(chips, tokens, -1)

    dl, hidden_parts = None, []
    for n in range(CHUNKS):
        parts = mapped_parts(tab, sources[n], align_tiles, chips)
        parts = [parts[0]] + [swap(parts[j], "dp", 2 * j) for j in range(1, chips)]
        dl, *terms = grads(n, core, e, a, b, weight_own, weight_other, parts, dl)
        others = [swap(terms[j], "dp", 2 * j) for j in range(1, chips)]
        rows_sum = sum([x.astype(F32) for x in others], terms[0].astype(F32))
        rows_sum = rows_sum.astype(BF16).reshape(2, -1, chips, features // dp).transpose(1, 2, 0, 3)
        pieces = rows_sum.reshape(-1, vocab, features // vocab).transpose(1, 0, 2)
        piece = lambda t: lax.dynamic_index_in_dim(pieces, v ^ t, 0, keepdims=False)
        part = piece(0).astype(F32)
        for t in range(1, vocab):
            part += swap(piece(t), "vocab", t).astype(F32)
        hidden_parts.append(part.astype(BF16))
    hidden_grad = jnp.concatenate(hidden_parts)
    dl = dl.reshape(chips * tokens, -1)

    def head_half(half):
        x = lax.dynamic_index_in_dim(hidden, half, 0, keepdims=False)
        return lax.dot_general(x, dl, (((0,), (0,)), ((), ())), preferred_element_type=F32).astype(BF16)

    half = head_half(1 - c)
    got = swap(half, "dp", 1)
    head_terms = (head_half(c).astype(F32) + got.astype(F32)).astype(BF16)
    head_grad = lax.all_to_all(
        head_terms, "dp", split_axis=0, concat_axis=1, axis_index_groups=groups, tiled=True
    )
    return (hidden_grad, head_grad)


def solution(mesh):
    placed = (
        P("dp", None),
        P("dp", "vocab"),
        P("dp", "vocab"),
        P(),
        P("vocab", None, None, None),
        P("dp"),
    )
    return jax.shard_map(
        body,
        mesh=mesh,
        in_specs=placed,
        out_specs=(P("dp", "vocab"), P("dp", "vocab")),
        check_vma=False,
    )
```

```python
import functools

import jax
import jax.numpy as jnp
from jax import lax
from jax.experimental import pallas as pl
from jax.experimental.pallas import tpu as pltpu
from jax.sharding import PartitionSpec as P


BLOCK = 128
K = 2
HALVES = 2

ANY = pl.BlockSpec(memory_space=pl.ANY)
VMEM = pl.BlockSpec(memory_space=pltpu.VMEM)
F32 = jnp.float32
BF16 = jnp.bfloat16


def swap(x, axis, bits):
    return lax.ppermute(x, axis, [(i, i ^ bits) for i in range(lax.axis_size(axis))])


def probs_kernel(x_ref, out_ref):
    rows = out_ref.shape[2]
    for j in range(out_ref.shape[1]):
        block = jnp.exp(x_ref[:, j * BLOCK : (j + 1) * BLOCK]).astype(BF16)
        for n in range(HALVES):
            out_ref[n, j] = block[n * rows : (n + 1) * rows]


def teacher_blocks(logprobs):
    tokens, cols = logprobs.shape
    count = cols // BLOCK
    step = next(s for s in (8, 5, 4, 2, 1) if count % s == 0)
    rows = tokens // HALVES
    return pl.pallas_call(
        probs_kernel,
        grid=(count // step,),
        in_specs=[pl.BlockSpec((tokens, step * BLOCK), lambda i: (0, i))],
        out_specs=pl.BlockSpec((HALVES, step, rows, BLOCK), lambda i: (0, i, 0, 0)),
        out_shape=jax.ShapeDtypeStruct((HALVES, count, rows, BLOCK), BF16),
        name="probs",
    )(logprobs)


def flatten(sources):
    flat, views = [], []
    for source in sources:
        split = isinstance(source, list)
        views.append((len(flat), split))
        flat += source if split else [source]
    return flat, views


def half_of(refs, view, n):
    at, split = view
    return refs[at + n] if split else refs[at].at[n]


def pack_kernel(first, halves, views, vocab, tab_ref, *refs):
    out_ref, sem = refs[-2], refs[-1]
    v = tab_ref[6, 0]
    row = jnp.where(v == 1, 0, 1)

    def start(slot, carry):
        far, block = tab_ref[2 + row, first + slot], tab_ref[4 + row, first + slot]
        for i, view in enumerate(views):

            @pl.when(far == i + 1)
            def _(view=view):
                for k, n in enumerate(halves):
                    pltpu.make_async_copy(half_of(refs, view, n).at[block], out_ref.at[k, slot], sem).start()

        return carry

    @pl.when((v == 1) | (v == vocab - 2))
    def _():
        lax.fori_loop(0, out_ref.shape[1], start, 0)
        pltpu.make_async_copy(out_ref, out_ref, sem).wait()


def pack(tab, first, capacity, sources, halves, vocab):
    flat, views = flatten(sources)
    return pl.pallas_call(
        functools.partial(pack_kernel, first, halves, views, vocab),
        grid_spec=pltpu.PrefetchScalarGridSpec(
            num_scalar_prefetch=1,
            grid=(),
            in_specs=[ANY] * len(flat),
            out_specs=VMEM,
            scratch_shapes=[pltpu.SemaphoreType.DMA],
        ),
        out_shape=jax.ShapeDtypeStruct((len(halves), capacity) + flat[0].shape[-2:], BF16),
        name="pack",
    )(tab, *flat)


def mapped_kernel(pieces, views, tab_ref, *refs):
    tiles_ref, outs, buf, sem = refs[-len(pieces) - 3], refs[-len(pieces) - 2 : -2], refs[-2], refs[-1]
    me = tab_ref[6, 1]
    per = outs[0].shape[1] // BLOCK
    entries = per * K
    rows = buf.shape[1] // HALVES

    for at, piece in enumerate(pieces):
        base = lax.bitwise_xor(me, piece) * entries

        def start(p, carry, at=at, base=base):
            source, block = tab_ref[0, base + p], tab_ref[1, base + p]
            for i, view in enumerate(views):

                @pl.when(source == i)
                def _(view=view):
                    for n in range(HALVES):
                        pltpu.make_async_copy(
                            half_of(refs, view, n).at[block],
                            buf.at[at * entries + p, pl.ds(n * rows, rows)],
                            sem,
                        ).start()

            return carry

        lax.fori_loop(0, entries, start, 0)
    pltpu.make_async_copy(buf, buf, sem).wait()
    for at, (piece, out) in enumerate(zip(pieces, outs)):
        dest = lax.bitwise_xor(me, piece)
        for j in range(per):
            p = at * entries + K * j
            total = jnp.dot(buf[p], tiles_ref[dest * per + j, 0], preferred_element_type=F32)
            for k in range(1, K):
                total += jnp.dot(buf[p + k], tiles_ref[dest * per + j, k], preferred_element_type=F32)
            out[:, j * BLOCK : (j + 1) * BLOCK] = total.astype(BF16)


def mapped_parts(tab, sources, tiles, chips, pieces):
    flat, views = flatten(sources)
    tokens = HALVES * flat[0].shape[-2]
    cols = tiles.shape[0] * BLOCK // chips
    return pl.pallas_call(
        functools.partial(mapped_kernel, pieces, views),
        grid_spec=pltpu.PrefetchScalarGridSpec(
            num_scalar_prefetch=1,
            grid=(),
            in_specs=[ANY] * len(flat) + [VMEM],
            out_specs=[VMEM] * len(pieces),
            scratch_shapes=[
                pltpu.VMEM((len(pieces) * cols // BLOCK * K, tokens, BLOCK), BF16),
                pltpu.SemaphoreType.DMA,
            ],
        ),
        out_shape=[jax.ShapeDtypeStruct((tokens, cols), BF16)] * len(pieces),
        name="mapped",
    )(tab, *flat, tiles)


def turned(x):
    n = max(x.shape)
    full = jnp.broadcast_to(x, (n, n)).T
    return full[:, :1] if x.shape[0] == 1 else full[:1]


def logits_kernel(core_ref, x_ref, own_ref, other_ref, e_ref, s_ref):
    i, c = pl.program_id(0), core_ref[0]
    logits = jnp.dot(x_ref[c], own_ref[...], preferred_element_type=F32)
    logits += jnp.dot(x_ref[1 - c], other_ref[...], preferred_element_type=F32)
    top = jnp.max(logits, axis=1, keepdims=True)
    e = jnp.exp(logits - top)
    e_ref[0] = e
    s_ref[0, pl.ds(i, 1)] = turned(top)
    s_ref[1, pl.ds(i, 1)] = turned(jnp.sum(e, axis=1, keepdims=True))


def logits_parts(core, hidden, own, other, tokens):
    chips = hidden.shape[1] // tokens
    features, cols = own.shape
    fixed = pl.BlockSpec((features, cols), lambda i, core: (0, 0))
    return pl.pallas_call(
        logits_kernel,
        grid_spec=pltpu.PrefetchScalarGridSpec(
            num_scalar_prefetch=1,
            grid=(chips,),
            in_specs=[pl.BlockSpec((2, tokens, features), lambda i, core: (0, i, 0)), fixed, fixed],
            out_specs=[
                pl.BlockSpec((1, tokens, cols), lambda i, core: (i, 0, 0)),
                pl.BlockSpec((2, chips, tokens), lambda i, core: (0, 0, 0)),
            ],
        ),
        out_shape=[
            jax.ShapeDtypeStruct((chips, tokens, cols), F32),
            jax.ShapeDtypeStruct((2, chips, tokens), F32),
        ],
        name="logits",
    )(core, hidden, own, other)


def stats_kernel(order, own_ref, *refs):
    shares, a_ref, b_ref = refs[:-2], refs[-2], refs[-1]
    chips = len(shares)
    for k, piece in enumerate(order):
        rows = [order.index(piece ^ r) for r in range(chips)]
        tops = [shares[r][j : j + 1] for r, j in enumerate(rows)]
        top = functools.reduce(jnp.maximum, tops)
        total = sum(shares[r][chips + j : chips + j + 1] * jnp.exp(tops[r] - top) for r, j in enumerate(rows))
        mass = shares[piece][2 * chips : 2 * chips + 1]
        scale = shares[piece][2 * chips + 1 : 2 * chips + 2]
        a_ref[k] = turned(scale * mass * (jnp.exp(own_ref[0, k : k + 1] - top) / total))
        b_ref[k] = turned(scale)


def grads_kernel(core_ref, e_ref, a_ref, b_ref, own_ref, other_ref, *refs):
    count = e_ref.shape[0]
    mapped, dl_ref, outs = refs[:count], refs[-count - 1], refs[-count:]
    c = core_ref[0]
    for k in range(count):
        dl = (a_ref[k] * e_ref[k] - b_ref[k] * mapped[k][...].astype(F32)).astype(BF16)
        dl_ref[k] = dl
        for half, weight in ((c, own_ref), (1 - c, other_ref)):
            terms = lax.dot_general(dl, weight[...], (((1,), (1,)), ((), ())), preferred_element_type=F32)
            outs[k][half] = terms.astype(BF16)


def grads(part, core, e, a, b, own, other, mapped, dl):
    count, tokens = len(mapped), mapped[0].shape[0]
    features, cols = own.shape
    some = lambda n: pl.BlockSpec((count, tokens, n), lambda i, core: (part, 0, 0))
    whole = lambda *shape: pl.BlockSpec(shape, lambda i, core: (0,) * len(shape))
    return pl.pallas_call(
        grads_kernel,
        grid_spec=pltpu.PrefetchScalarGridSpec(
            num_scalar_prefetch=1,
            grid=(1,),
            in_specs=[some(cols), some(1), some(1), whole(features, cols), whole(features, cols)]
            + [whole(tokens, cols)] * count
            + ([] if dl is None else [ANY]),
            out_specs=[some(cols)] + [whole(2, tokens, features)] * count,
        ),
        out_shape=[jax.ShapeDtypeStruct(e.shape, BF16)]
        + [jax.ShapeDtypeStruct((2, tokens, features), BF16)] * count,
        input_output_aliases={} if dl is None else {6 + count: 0},
        name="grads",
    )(core, e, a, b, own, other, *mapped, *([] if dl is None else [dl]))


def body(student_hidden, head_weight, teacher_logprobs, align_index, align_tiles, grad_scale):
    vocab = lax.axis_size("vocab")
    dp = lax.axis_size("dp")
    v = lax.axis_index("vocab")
    d = lax.axis_index("dp")
    chips, chip, c = dp // 2, d // 2, d % 2
    core = c.astype(jnp.int32)[None]
    tokens, features = student_hidden.shape
    count = teacher_logprobs.shape[1] // BLOCK
    pairs = align_tiles.shape[0] * K
    capacity = (2 * pairs + vocab - 1) // vocab
    packs = (pairs + capacity - 1) // capacity
    if vocab < 4 or vocab & (vocab - 1) or dp & (dp - 1):
        raise ValueError("mesh sizes")
    groups = [[2 * i + j for i in range(chips)] for j in range(2)]

    blocks = teacher_blocks(teacher_logprobs)

    hops = [(r, i) for r in range(1, vocab - 1) for i in range(r - 1, vocab - 2)]
    number_of = [[0] * vocab for _ in range(vocab)]
    for i in range(1, vocab - 1):
        for o in range(vocab):
            if o != i:
                link = i - 1 if o < i else vocab - 2 - i
                number_of[i][o] = 1 + hops.index((abs(o - i), link))

    rows = align_index.reshape(vocab, pairs)
    ends = jnp.stack([rows[0], rows[vocab - 1]])
    end_owner, end_local = lax.div(ends, jnp.int32(count)), lax.rem(ends, jnp.int32(count))
    end_far = jnp.abs(end_owner - jnp.array([[0], [vocab - 1]]))
    number = jnp.arange(pairs)
    later = (end_far[:, None, :] > end_far[:, :, None]) | (
        (end_far[:, None, :] == end_far[:, :, None]) & (number[None, None, :] >= number[None, :, None])
    )
    end_slot = packs * capacity - jnp.sum((later & (end_far[:, None, :] > 0)).astype(jnp.int32), axis=2)
    end_slot = jnp.where(end_far > 0, end_slot, -1)
    own = lax.dynamic_index_in_dim(rows, v, 0, keepdims=False)
    own_owner, own_local = lax.div(own, jnp.int32(count)), lax.rem(own, jnp.int32(count))
    own_slot = jnp.where(v == 0, end_slot[0], end_slot[1])
    at_end = ((v == 0) | (v == vocab - 1)) & (own_owner != v)
    numbers = lax.dynamic_index_in_dim(jnp.array(number_of, jnp.int32), v, 0, keepdims=False)
    source = jnp.sum(
        jnp.where(own_owner[None, :] == jnp.arange(vocab)[:, None], numbers[:, None], 0), axis=0
    )
    source = jnp.where(at_end, 1 + len(hops) + lax.div(own_slot, jnp.int32(capacity)), source)
    place = jnp.where(at_end, lax.rem(own_slot, jnp.int32(capacity)), own_local)
    me = jnp.where(number == 0, v, chip)
    filled = (end_slot[:, None, :] == number[None, :, None]).astype(jnp.int32)
    slot_far = jnp.maximum(jnp.sum(filled * end_far[:, None, :], axis=2), 1)
    slot_local = jnp.sum(filled * end_local[:, None, :], axis=2)
    tab = jnp.concatenate([source[None], place[None], slot_far, slot_local, me[None]], axis=0).astype(jnp.int32)

    def hop(x, i):
        return lax.ppermute(x, "vocab", [(i, i + 1), (vocab - 1 - i, vocab - 2 - i)])

    moved = {(0, i): blocks for i in range(-1, vocab)}
    for r, i in hops:
        x = moved[r - 1, i - 1]
        if r == 1:
            moved[r, i] = hop(x, i)
        else:
            moved[r, i] = [hop(x[n], i) for n in range(HALVES)]
    near = [blocks] + [moved[r, vocab - 3] for r in range(1, vocab - 1)]

    def last(q, halves):
        part = pack(tab, q * capacity, capacity, near[: q - packs + vocab], halves, vocab)
        return lax.ppermute(part, "vocab", [(vocab - 2, vocab - 1), (1, 0)])

    packed = [last(q, range(HALVES)) for q in range(packs - 1)]
    packed.append([last(packs - 1, [n])[0] for n in range(HALVES)])
    sources = [blocks] + [moved[h] for h in hops] + packed

    weight_own = lax.all_to_all(head_weight, "dp", split_axis=1, concat_axis=0, axis_index_groups=groups, tiled=True)
    weight_other = swap(weight_own, "dp", 1)

    hidden = student_hidden.reshape(tokens, chips, 2, features // dp).transpose(2, 0, 1, 3)
    hidden = hidden.reshape(2, tokens, features // 2)
    others = [swap(hidden, "dp", 2 * j) for j in range(1, chips)]
    order = list(range(chips))[::-1]
    hidden = jnp.concatenate(others[::-1] + [hidden], axis=1)
    e, local = logits_parts(core, hidden, weight_own, weight_other, tokens)

    row_sums = jnp.sum(align_tiles.astype(F32), axis=3).reshape(pairs, BLOCK)
    all_sums = [row_sums] + [swap(row_sums, "vocab", t) for t in range(1, vocab)]
    all_rows = [own] + [lax.dynamic_index_in_dim(rows, v ^ t, 0, keepdims=False) for t in range(1, vocab)]
    hits = (jnp.concatenate(all_rows)[None, :] == (v * count + jnp.arange(count))[:, None]).astype(F32)
    entry_weight = jnp.dot(hits, jnp.concatenate(all_sums), precision=lax.Precision.HIGHEST)
    mass = jnp.sum(blocks.astype(F32) * entry_weight[None, :, None, :], axis=(1, 3)).reshape(tokens)

    share = jnp.concatenate([local.reshape(2 * chips, tokens), mass[None]])
    shares = [share] + [swap(share, "vocab", t) for t in range(1, vocab)]
    plane_top = functools.reduce(jnp.maximum, [s[:chips] for s in shares])
    plane_total = sum(s[chips : 2 * chips] * jnp.exp(s[:chips] - plane_top) for s in shares)
    plane_mass = sum(s[2 * chips] for s in shares)
    share = jnp.concatenate([plane_top, plane_total, plane_mass[None], grad_scale[None]])
    shares = [share] + [swap(share, "dp", 2 * j) for j in range(1, chips)]
    column = jax.ShapeDtypeStruct((chips, tokens, 1), F32)
    a, b = pl.pallas_call(
        functools.partial(stats_kernel, order),
        in_specs=[VMEM] * (chips + 1),
        out_specs=[VMEM, VMEM],
        out_shape=[column, column],
        name="stats",
    )(local, *shares)

    count = chips // 2
    columns, terms, dl = [], [], None
    for n in range(2):
        pieces = order[n * count : (n + 1) * count]
        parts = mapped_parts(tab, sources, align_tiles, chips, pieces)
        columns.append([x if j == 0 else swap(x, "dp", 2 * j) for x, j in zip(parts, pieces)])
    for n in range(2):
        pieces = order[n * count : (n + 1) * count]
        dl, *parts = grads(n, core, e, a, b, weight_own, weight_other, columns[n], dl)
        terms += [x if j == 0 else swap(x, "dp", 2 * j) for x, j in zip(parts, pieces)]
    rows_sum = sum([x.astype(F32) for x in terms[:-1]], terms[-1].astype(F32))
    rows_sum = rows_sum.astype(BF16).reshape(2, -1, chips, features // dp).transpose(1, 2, 0, 3)
    pieces = rows_sum.reshape(-1, vocab, features // vocab).transpose(1, 0, 2)
    piece = lambda t: lax.dynamic_index_in_dim(pieces, v ^ t, 0, keepdims=False)
    hidden_grad = piece(0).astype(F32)
    others = [swap(piece(t), "vocab", t) for t in range(1, vocab)]
    hidden_grad = sum([x.astype(F32) for x in others], hidden_grad).astype(BF16)
    dl = dl.reshape(chips * tokens, -1)

    def head_half(half):
        x = lax.dynamic_index_in_dim(hidden, half, 0, keepdims=False)
        return lax.dot_general(x, dl, (((0,), (0,)), ((), ())), preferred_element_type=F32).astype(BF16)

    half = head_half(1 - c)
    got = swap(half, "dp", 1)
    head_terms = (head_half(c).astype(F32) + got.astype(F32)).astype(BF16)
    head_grad = lax.all_to_all(
        head_terms, "dp", split_axis=0, concat_axis=1, axis_index_groups=groups, tiled=True
    )
    return (hidden_grad, head_grad)


def solution(mesh):
    placed = (
        P("dp", None),
        P("dp", "vocab"),
        P("dp", "vocab"),
        P(),
        P("vocab", None, None, None),
        P("dp"),
    )
    return jax.shard_map(
        body,
        mesh=mesh,
        in_specs=placed,
        out_specs=(P("dp", "vocab"), P("dp", "vocab")),
        check_vma=False,
    )
```

```python
import functools

import jax
import jax.numpy as jnp
from jax import lax
from jax.experimental import pallas as pl
from jax.experimental.pallas import tpu as pltpu
from jax.sharding import PartitionSpec as P


BLOCK = 128
K = 2
SPLIT = (64, 64)
HALVES = len(SPLIT)

ANY = pl.BlockSpec(memory_space=pl.ANY)
VMEM = pl.BlockSpec(memory_space=pltpu.VMEM)
F32 = jnp.float32
BF16 = jnp.bfloat16


def swap(x, axis, bits):
    return lax.ppermute(x, axis, [(i, i ^ bits) for i in range(lax.axis_size(axis))])


def parts_of(tokens):
    return [tokens * sum(SPLIT[:n]) // sum(SPLIT) for n in range(HALVES + 1)]


def probs_kernel(peers, tab_ref, x_ref, *out_refs):
    count = len(out_refs) // HALVES
    ends = parts_of(x_ref.shape[0])

    def block(at):
        return jnp.exp(x_ref[:, pl.ds(pl.multiple_of(at * BLOCK, BLOCK), BLOCK)]).astype(BF16)

    def store(list_number, slot, value):
        for n in range(HALVES):
            out_refs[n * count + list_number][slot] = value[ends[n] : ends[n + 1]]

    def convert(slot, carry):
        store(0, slot, block(slot))
        return carry

    lax.fori_loop(0, out_refs[0].shape[0], convert, 0)
    for t in range(1, peers):

        def copy(slot, carry, t=t):
            at = tab_ref[2 + t, slot]
            for n in range(HALVES):
                out_refs[n * count + t][slot] = out_refs[n * count][at]
            return carry

        lax.fori_loop(0, out_refs[t].shape[0], copy, 0)


def teacher_lists(tab, logprobs, peers, length):
    tokens, cols = logprobs.shape
    ends = parts_of(tokens)
    lengths = [cols // BLOCK] + [length] * (peers - 1)
    shapes = [(n, y - x, BLOCK) for x, y in zip(ends, ends[1:]) for n in lengths]
    return pl.pallas_call(
        functools.partial(probs_kernel, peers),
        grid_spec=pltpu.PrefetchScalarGridSpec(
            num_scalar_prefetch=1, grid=(), in_specs=[VMEM], out_specs=[VMEM] * len(shapes)
        ),
        out_shape=[jax.ShapeDtypeStruct(shape, BF16) for shape in shapes],
        name="probs",
    )(tab, logprobs)


def mapped_kernel(pieces, tab_ref, *refs):
    sources, tiles_ref, outs = refs[: -len(pieces) - 3], refs[-len(pieces) - 3], refs[-len(pieces) - 2 : -2]
    buf, sem = refs[-2], refs[-1]
    me = tab_ref[2, 0]
    per = outs[0].shape[1] // BLOCK

    def start(p, carry):
        source, block = tab_ref[0, p], tab_ref[1, p]
        for i, ref in enumerate(sources):

            @pl.when(source == i)
            def _(ref=ref):
                pltpu.make_async_copy(ref.at[block], buf.at[p], sem).start()

        return carry

    lax.fori_loop(0, buf.shape[0], start, 0)
    pltpu.make_async_copy(buf, buf, sem).wait()
    for piece, out in zip(pieces, outs):
        dest = lax.bitwise_xor(me, piece)
        for j in range(per):
            b = dest * per + j
            total = jnp.dot(buf[K * b], tiles_ref[b, 0], preferred_element_type=F32)
            for k in range(1, K):
                total += jnp.dot(buf[K * b + k], tiles_ref[b, k], preferred_element_type=F32)
            out[:, j * BLOCK : (j + 1) * BLOCK] = total.astype(BF16)


def mapped_parts(tab, sources, tiles, pieces):
    rows = sources[0].shape[1]
    cols = tiles.shape[0] * BLOCK // len(pieces)
    return pl.pallas_call(
        functools.partial(mapped_kernel, pieces),
        grid_spec=pltpu.PrefetchScalarGridSpec(
            num_scalar_prefetch=1,
            grid=(),
            in_specs=[ANY] * len(sources) + [VMEM],
            out_specs=[VMEM] * len(pieces),
            scratch_shapes=[pltpu.VMEM((tab.shape[1], rows, BLOCK), BF16), pltpu.SemaphoreType.DMA],
        ),
        out_shape=[jax.ShapeDtypeStruct((rows, cols), BF16)] * len(pieces),
        name="mapped",
    )(tab, *sources, tiles)


def turned(x):
    n = max(x.shape)
    full = jnp.broadcast_to(x, (n, n)).T
    return full[:, :1] if x.shape[0] == 1 else full[:1]


def logits_kernel(core_ref, x_ref, own_ref, other_ref, e_ref, s_ref):
    i, c = pl.program_id(0), core_ref[0]
    logits = jnp.dot(x_ref[c], own_ref[...], preferred_element_type=F32)
    logits += jnp.dot(x_ref[1 - c], other_ref[...], preferred_element_type=F32)
    top = jnp.max(logits, axis=1, keepdims=True)
    e = jnp.exp(logits - top)
    e_ref[0] = e
    s_ref[0, pl.ds(i, 1)] = turned(top)
    s_ref[1, pl.ds(i, 1)] = turned(jnp.sum(e, axis=1, keepdims=True))


def logits_parts(core, hidden, own, other, tokens):
    chips = hidden.shape[1] // tokens
    features, cols = own.shape
    fixed = pl.BlockSpec((features, cols), lambda i, core: (0, 0))
    return pl.pallas_call(
        logits_kernel,
        grid_spec=pltpu.PrefetchScalarGridSpec(
            num_scalar_prefetch=1,
            grid=(chips,),
            in_specs=[pl.BlockSpec((2, tokens, features), lambda i, core: (0, i, 0)), fixed, fixed],
            out_specs=[
                pl.BlockSpec((1, tokens, cols), lambda i, core: (i, 0, 0)),
                pl.BlockSpec((2, chips, tokens), lambda i, core: (0, 0, 0)),
            ],
        ),
        out_shape=[
            jax.ShapeDtypeStruct((chips, tokens, cols), F32),
            jax.ShapeDtypeStruct((2, chips, tokens), F32),
        ],
        name="logits",
    )(core, hidden, own, other)


def stats_kernel(order, own_ref, *refs):
    shares, a_ref, b_ref = refs[:-2], refs[-2], refs[-1]
    chips = len(shares)
    for k, piece in enumerate(order):
        rows = [order.index(piece ^ r) for r in range(chips)]
        tops = [shares[r][j : j + 1] for r, j in enumerate(rows)]
        top = functools.reduce(jnp.maximum, tops)
        total = sum(shares[r][chips + j : chips + j + 1] * jnp.exp(tops[r] - top) for r, j in enumerate(rows))
        mass = shares[piece][2 * chips : 2 * chips + 1]
        scale = shares[piece][2 * chips + 1 : 2 * chips + 2]
        a_ref[k] = turned(scale * mass * (jnp.exp(own_ref[0, k : k + 1] - top) / total))
        b_ref[k] = turned(scale)


def grads_kernel(core_ref, e_ref, a_ref, b_ref, own_ref, other_ref, *refs):
    count = e_ref.shape[0]
    mapped, dl_ref, outs = refs[:count], refs[-count - 1], refs[-count:]
    c = core_ref[0]
    for k in range(count):
        dl_ref[k] = (a_ref[k] * e_ref[k] - b_ref[k] * mapped[k][...].astype(F32)).astype(BF16)
    rows = dl_ref.shape[1]
    dl = dl_ref[...].reshape(count * rows, -1)
    for half, weight in ((c, own_ref), (1 - c, other_ref)):
        terms = lax.dot_general(dl, weight[...], (((1,), (1,)), ((), ())), preferred_element_type=F32)
        for k in range(count):
            outs[k][half] = terms[k * rows : (k + 1) * rows].astype(BF16)


def grads(part, core, e, a, b, own, other, mapped, dl):
    count, rows = len(mapped), mapped[0].shape[0]
    features, cols = own.shape
    at = parts_of(e.shape[1])[part] // rows
    some = lambda n: pl.BlockSpec((count, rows, n), lambda i, core: (0, at, 0))
    whole = lambda *shape: pl.BlockSpec(shape, lambda i, core: (0,) * len(shape))
    return pl.pallas_call(
        grads_kernel,
        grid_spec=pltpu.PrefetchScalarGridSpec(
            num_scalar_prefetch=1,
            grid=(1,),
            in_specs=[some(cols), some(1), some(1), whole(features, cols), whole(features, cols)]
            + [whole(rows, cols)] * count
            + ([] if dl is None else [ANY]),
            out_specs=[some(cols)] + [whole(2, rows, features)] * count,
        ),
        out_shape=[jax.ShapeDtypeStruct(e.shape, BF16)]
        + [jax.ShapeDtypeStruct((2, rows, features), BF16)] * count,
        input_output_aliases={} if dl is None else {6 + count: 0},
        name="grads",
    )(core, e, a, b, own, other, *mapped, *([] if dl is None else [dl]))


def plan(align_index, pairs, count, chip):
    vocab = lax.axis_size("vocab")
    v = lax.axis_index("vocab")
    rows = align_index.reshape(vocab, pairs)
    owner, local = lax.div(rows, jnp.int32(count)), lax.rem(rows, jnp.int32(count))
    number = jnp.arange(pairs)
    same = rows[:, :, None] == rows[:, None, :]
    first = ~jnp.any(same & (number[None, None, :] < number[None, :, None]), axis=2)
    less = (owner[:, :, None] == owner[:, None, :]) & (rows[:, None, :] < rows[:, :, None]) & first[:, None, :]
    rank = jnp.sum(less.astype(jnp.int32), axis=2)
    here = jnp.arange(vocab)[:, None]
    longest = jnp.max(jnp.where(owner != here, rank + 1, 0))
    pick = lambda x, i: lax.dynamic_index_in_dim(x, i, 0, keepdims=False)
    own_owner = pick(owner, v)
    source = own_owner ^ v
    place = jnp.where(own_owner == v, pick(local, v), pick(rank, v))
    asked = (owner == v)[:, None, :] & (rank[:, None, :] == number[None, :, None]) & first[:, None, :]
    lists = jnp.sum(jnp.where(asked, local[:, None, :], 0), axis=2)
    mine = jnp.where(number == 0, chip, 0)
    tab = jnp.stack([source, place, mine] + [pick(lists, v ^ t) for t in range(1, vocab)])
    return tab.astype(jnp.int32), longest


def body(student_hidden, head_weight, teacher_logprobs, align_index, align_tiles, grad_scale):
    vocab = lax.axis_size("vocab")
    chips = lax.axis_size("dp") // 2
    count = teacher_logprobs.shape[1] // BLOCK
    pairs = align_tiles.shape[0] * K
    capacity = (2 * pairs + vocab - 1) // vocab
    if vocab & (vocab - 1) or chips & (chips - 1):
        raise ValueError("mesh sizes")
    tab, longest = plan(align_index, pairs, count, lax.axis_index("dp") // 2)
    operands = (student_hidden, head_weight, teacher_logprobs, align_index, align_tiles, grad_scale, tab)
    lengths = (3 * capacity // 4, capacity)

    def branch(n):
        def run(*args):
            return step(lengths[n], *args)

        return run

    return lax.cond(longest <= lengths[0], branch(0), branch(1), *operands)


def step(length, student_hidden, head_weight, teacher_logprobs, align_index, align_tiles, grad_scale, tab):
    vocab = lax.axis_size("vocab")
    dp = lax.axis_size("dp")
    v = lax.axis_index("vocab")
    d = lax.axis_index("dp")
    chips, c = dp // 2, d % 2
    core = c.astype(jnp.int32)[None]
    tokens, features = student_hidden.shape
    count = teacher_logprobs.shape[1] // BLOCK
    pairs = align_tiles.shape[0] * K
    groups = [[2 * i + j for i in range(chips)] for j in range(2)]

    lists = teacher_lists(tab, teacher_logprobs, vocab, length)
    lists = [lists[n * vocab : (n + 1) * vocab] for n in range(HALVES)]
    blocks, sources = [x[0] for x in lists], []
    for n in range(HALVES):
        got = []
        for t in range(1, vocab):
            got.append(swap(lists[n][t], "vocab", t))
        sources.append([blocks[n]] + got)

    weight_own = lax.all_to_all(head_weight, "dp", split_axis=1, concat_axis=0, axis_index_groups=groups, tiled=True)
    weight_other = swap(weight_own, "dp", 1)

    hidden = student_hidden.reshape(tokens, chips, 2, features // dp).transpose(2, 0, 1, 3)
    hidden = lax.optimization_barrier(hidden.reshape(2, tokens, features // 2))
    others = [swap(hidden, "dp", 2 * j) for j in range(1, chips)]
    order = list(range(chips))[::-1]
    hidden = jnp.concatenate(others[::-1] + [hidden], axis=1)
    e, local = logits_parts(core, hidden, weight_own, weight_other, tokens)

    row_sums = jnp.sum(align_tiles.astype(F32), axis=3).reshape(pairs, BLOCK)
    all_sums = [row_sums] + [swap(row_sums, "vocab", t) for t in range(1, vocab)]
    rows = align_index.reshape(vocab, pairs)
    all_rows = [lax.dynamic_index_in_dim(rows, v ^ t, 0, keepdims=False) for t in range(vocab)]
    hits = (jnp.concatenate(all_rows)[None, :] == (v * count + jnp.arange(count))[:, None]).astype(F32)
    entry_weight = jnp.dot(hits, jnp.concatenate(all_sums), precision=lax.Precision.HIGHEST)
    mass = jnp.concatenate(
        [jnp.sum(part.astype(F32) * entry_weight[:, None, :], axis=(0, 2)) for part in blocks]
    )

    share = jnp.concatenate([local.reshape(2 * chips, tokens), mass[None]])
    shares = [share] + [swap(share, "vocab", t) for t in range(1, vocab)]
    plane_top = functools.reduce(jnp.maximum, [s[:chips] for s in shares])
    plane_total = sum(s[chips : 2 * chips] * jnp.exp(s[:chips] - plane_top) for s in shares)
    plane_mass = sum(s[2 * chips] for s in shares)
    share = jnp.concatenate([plane_top, plane_total, plane_mass[None], grad_scale[None]])
    shares = [share] + [swap(share, "dp", 2 * j) for j in range(1, chips)]
    column = jax.ShapeDtypeStruct((chips, tokens, 1), F32)
    a, b = pl.pallas_call(
        functools.partial(stats_kernel, order),
        in_specs=[VMEM] * (chips + 1),
        out_specs=[VMEM, VMEM],
        out_shape=[column, column],
        name="stats",
    )(local, *shares)

    dl, hidden_parts = None, []
    for n in range(HALVES):
        parts = mapped_parts(tab, sources[n], align_tiles, order)
        parts = [x if j == 0 else swap(x, "dp", 2 * j) for x, j in zip(parts, order)]
        dl, *terms = grads(n, core, e, a, b, weight_own, weight_other, parts, dl)
        terms = [x if j == 0 else swap(x, "dp", 2 * j) for x, j in zip(terms, order)]
        rows_sum = sum([x.astype(F32) for x in terms[:-1]], terms[-1].astype(F32))
        rows_sum = rows_sum.astype(BF16).reshape(2, -1, chips, features // dp).transpose(1, 2, 0, 3)
        pieces = rows_sum.reshape(-1, vocab, features // vocab).transpose(1, 0, 2)
        hidden_parts.append(pieces)
    pieces = jnp.concatenate(hidden_parts, axis=1)
    piece = lambda t: lax.dynamic_index_in_dim(pieces, v ^ t, 0, keepdims=False)
    hidden_grad = piece(0).astype(F32)
    others = [swap(piece(t), "vocab", t) for t in range(1, vocab)]
    hidden_grad = sum([x.astype(F32) for x in others], hidden_grad).astype(BF16)
    dl = dl.reshape(chips * tokens, -1)

    def head_half(half):
        x = lax.dynamic_index_in_dim(hidden, half, 0, keepdims=False)
        return lax.dot_general(x, dl, (((0,), (0,)), ((), ())), preferred_element_type=F32).astype(BF16)

    half = head_half(1 - c)
    got = swap(half, "dp", 1)
    half = head_half(c)
    head_terms = (half.astype(F32) + got.astype(F32)).astype(BF16)
    head_grad = lax.all_to_all(
        head_terms, "dp", split_axis=0, concat_axis=1, axis_index_groups=groups, tiled=True
    )
    return (hidden_grad, head_grad)


def solution(mesh):
    placed = (
        P("dp", None),
        P("dp", "vocab"),
        P("dp", "vocab"),
        P(),
        P("vocab", None, None, None),
        P("dp"),
    )
    return jax.shard_map(
        body,
        mesh=mesh,
        in_specs=placed,
        out_specs=(P("dp", "vocab"), P("dp", "vocab")),
        check_vma=False,
    )
```

```python
import functools

import jax
import jax.numpy as jnp
from jax import lax
from jax.experimental import pallas as pl
from jax.experimental.pallas import tpu as pltpu
from jax.sharding import PartitionSpec as P


BLOCK = 128
K = 2
SPLIT = (64, 64)
HALVES = len(SPLIT)

ANY = pl.BlockSpec(memory_space=pl.ANY)
VMEM = pl.BlockSpec(memory_space=pltpu.VMEM)
F32 = jnp.float32
BF16 = jnp.bfloat16


def swap(x, axis, bits):
    return lax.ppermute(x, axis, [(i, i ^ bits) for i in range(lax.axis_size(axis))])


def parts_of(tokens):
    return [tokens * sum(SPLIT[:n]) // sum(SPLIT) for n in range(HALVES + 1)]


def probs_kernel(tab_ref, x_ref, own_ref, *out_refs):
    def convert(block, carry):
        columns = pl.ds(pl.multiple_of(block * BLOCK, BLOCK), BLOCK)
        own_ref[block] = jnp.exp(x_ref[:, columns]).astype(BF16)
        return carry

    lax.fori_loop(0, own_ref.shape[0], convert, 0, unroll=4)
    for t, out in enumerate(out_refs):

        def copy(slot, carry, t=t, out=out):
            out[slot] = own_ref[tab_ref[3 + t, slot]]
            return carry

        lax.fori_loop(0, out.shape[0], copy, 0, unroll=4)


def teacher_lists(part, tab, logprobs, lengths):
    tokens, cols = logprobs.shape
    ends = parts_of(tokens)
    rows = ends[part + 1] - ends[part]
    shapes = [(n, rows, BLOCK) for n in [cols // BLOCK] + lengths]
    whole = lambda shape: pl.BlockSpec(shape, lambda i, tab: (0, 0, 0))
    return pl.pallas_call(
        probs_kernel,
        grid_spec=pltpu.PrefetchScalarGridSpec(
            num_scalar_prefetch=1,
            grid=(1,),
            in_specs=[pl.BlockSpec((rows, cols), lambda i, tab: (ends[part] // rows, 0))],
            out_specs=[whole(shape) for shape in shapes],
        ),
        out_shape=[jax.ShapeDtypeStruct(shape, BF16) for shape in shapes],
        name="probs",
    )(tab, logprobs)


def mapped_kernel(pieces, tab_ref, *refs):
    sources, tiles_ref, outs = refs[: -len(pieces) - 3], refs[-len(pieces) - 3], refs[-len(pieces) - 2 : -2]
    buf, sem = refs[-2], refs[-1]
    me = tab_ref[2, 0]
    per = outs[0].shape[1] // BLOCK

    def start(p, carry):
        source, block = tab_ref[0, p], tab_ref[1, p]
        for i, ref in enumerate(sources):

            @pl.when(source == i)
            def _(ref=ref):
                pltpu.make_async_copy(ref.at[block], buf.at[p], sem).start()

        return carry

    lax.fori_loop(0, buf.shape[0], start, 0)
    pltpu.make_async_copy(buf, buf, sem).wait()
    for piece, out in zip(pieces, outs):
        dest = lax.bitwise_xor(me, piece)
        for j in range(per):
            b = dest * per + j
            total = jnp.dot(buf[K * b], tiles_ref[b, 0], preferred_element_type=F32)
            for k in range(1, K):
                total += jnp.dot(buf[K * b + k], tiles_ref[b, k], preferred_element_type=F32)
            out[:, j * BLOCK : (j + 1) * BLOCK] = total.astype(BF16)


def mapped_parts(tab, sources, tiles, pieces):
    rows = sources[0].shape[1]
    cols = tiles.shape[0] * BLOCK // len(pieces)
    return pl.pallas_call(
        functools.partial(mapped_kernel, pieces),
        grid_spec=pltpu.PrefetchScalarGridSpec(
            num_scalar_prefetch=1,
            grid=(),
            in_specs=[ANY] * len(sources) + [VMEM],
            out_specs=[VMEM] * len(pieces),
            scratch_shapes=[pltpu.VMEM((tab.shape[1], rows, BLOCK), BF16), pltpu.SemaphoreType.DMA],
        ),
        out_shape=[jax.ShapeDtypeStruct((rows, cols), BF16)] * len(pieces),
        name="mapped",
    )(tab, *sources, tiles)


def turned(x):
    n = max(x.shape)
    full = jnp.broadcast_to(x, (n, n)).T
    return full[:, :1] if x.shape[0] == 1 else full[:1]


def logits_kernel(core_ref, x_ref, own_ref, other_ref, e_ref, s_ref):
    i, c = pl.program_id(0), core_ref[0]
    logits = jnp.dot(x_ref[c], own_ref[...], preferred_element_type=F32)
    logits += jnp.dot(x_ref[1 - c], other_ref[...], preferred_element_type=F32)
    top = jnp.max(logits, axis=1, keepdims=True)
    e = jnp.exp(logits - top)
    e_ref[0] = e
    s_ref[0, pl.ds(i, 1)] = turned(top)
    s_ref[1, pl.ds(i, 1)] = turned(jnp.sum(e, axis=1, keepdims=True))


def logits_parts(core, hidden, own, other, tokens):
    chips = hidden.shape[1] // tokens
    features, cols = own.shape
    fixed = pl.BlockSpec((features, cols), lambda i, core: (0, 0))
    return pl.pallas_call(
        logits_kernel,
        grid_spec=pltpu.PrefetchScalarGridSpec(
            num_scalar_prefetch=1,
            grid=(chips,),
            in_specs=[pl.BlockSpec((2, tokens, features), lambda i, core: (0, i, 0)), fixed, fixed],
            out_specs=[
                pl.BlockSpec((1, tokens, cols), lambda i, core: (i, 0, 0)),
                pl.BlockSpec((2, chips, tokens), lambda i, core: (0, 0, 0)),
            ],
        ),
        out_shape=[
            jax.ShapeDtypeStruct((chips, tokens, cols), F32),
            jax.ShapeDtypeStruct((2, chips, tokens), F32),
        ],
        name="logits",
    )(core, hidden, own, other)


def stats_kernel(order, own_ref, *refs):
    shares, a_ref, b_ref = refs[:-2], refs[-2], refs[-1]
    chips = len(shares)
    for k, piece in enumerate(order):
        rows = [order.index(piece ^ r) for r in range(chips)]
        tops = [shares[r][j : j + 1] for r, j in enumerate(rows)]
        top = functools.reduce(jnp.maximum, tops)
        total = sum(shares[r][chips + j : chips + j + 1] * jnp.exp(tops[r] - top) for r, j in enumerate(rows))
        mass = shares[piece][2 * chips : 2 * chips + 1]
        scale = shares[piece][2 * chips + 1 : 2 * chips + 2]
        a_ref[k] = turned(scale * mass * (jnp.exp(own_ref[0, k : k + 1] - top) / total))
        b_ref[k] = turned(scale)


def grads_kernel(core_ref, e_ref, a_ref, b_ref, own_ref, other_ref, *refs):
    count, tokens = e_ref.shape[:2]
    mapped, dl_ref, outs = refs[: HALVES * count], refs[-count - 1], refs[-count:]
    ends = parts_of(tokens)
    c = core_ref[0]
    for n in range(HALVES):
        some = slice(ends[n], ends[n + 1])
        for k in range(count):
            columns = mapped[n * count + k][...].astype(F32)
            dl_ref[k, some] = (a_ref[k, some] * e_ref[k, some] - b_ref[k, some] * columns).astype(BF16)
    dl = dl_ref[...].reshape(count * tokens, -1)
    for half, weight in ((c, own_ref), (1 - c, other_ref)):
        terms = lax.dot_general(dl, weight[...], (((1,), (1,)), ((), ())), preferred_element_type=F32)
        for k in range(count):
            outs[k][half] = terms[k * tokens : (k + 1) * tokens].astype(BF16)


def grads(core, e, a, b, own, other, mapped):
    count, tokens = e.shape[:2]
    return pl.pallas_call(
        grads_kernel,
        grid_spec=pltpu.PrefetchScalarGridSpec(
            num_scalar_prefetch=1,
            grid=(),
            in_specs=[VMEM] * (5 + len(mapped)),
            out_specs=[VMEM] * (1 + count),
        ),
        out_shape=[jax.ShapeDtypeStruct(e.shape, BF16)]
        + [jax.ShapeDtypeStruct((2, tokens, own.shape[0]), BF16)] * count,
        name="grads",
    )(core, e, a, b, own, other, *mapped)


def plan(align_index, pairs, count, chip):
    vocab = lax.axis_size("vocab")
    v = lax.axis_index("vocab")
    rows = align_index.reshape(vocab, pairs)
    owner, local = lax.div(rows, jnp.int32(count)), lax.rem(rows, jnp.int32(count))
    number = jnp.arange(pairs)
    same = rows[:, :, None] == rows[:, None, :]
    first = ~jnp.any(same & (number[None, None, :] < number[None, :, None]), axis=2)
    less = (owner[:, :, None] == owner[:, None, :]) & (rows[:, None, :] < rows[:, :, None]) & first[:, None, :]
    rank = jnp.sum(less.astype(jnp.int32), axis=2)
    here = jnp.arange(vocab)[:, None]
    longest = jnp.max(jnp.where((owner ^ here) >= vocab // 2, rank + 1, 0))
    pick = lambda x, i: lax.dynamic_index_in_dim(x, i, 0, keepdims=False)
    own_owner = pick(owner, v)
    source = own_owner ^ v
    place = jnp.where(own_owner == v, pick(local, v), pick(rank, v))
    asked = (owner == v)[:, None, :] & (rank[:, None, :] == number[None, :, None]) & first[:, None, :]
    lists = jnp.sum(jnp.where(asked, local[:, None, :], 0), axis=2)
    mine = jnp.where(number == 0, chip, 0)
    tab = jnp.stack([source, place, mine] + [pick(lists, v ^ t) for t in range(1, vocab)])
    return tab.astype(jnp.int32), longest


def body(student_hidden, head_weight, teacher_logprobs, align_index, align_tiles, grad_scale):
    vocab = lax.axis_size("vocab")
    chips = lax.axis_size("dp") // 2
    count = teacher_logprobs.shape[1] // BLOCK
    pairs = align_tiles.shape[0] * K
    capacity = (2 * pairs + vocab - 1) // vocab
    if vocab & (vocab - 1) or chips & (chips - 1):
        raise ValueError("mesh sizes")
    tab, longest = plan(align_index, pairs, count, lax.axis_index("dp") // 2)
    operands = (student_hidden, head_weight, teacher_logprobs, align_index, align_tiles, grad_scale, tab)
    lengths = (11 * capacity // 16, capacity)

    def branch(n):
        def run(*args):
            return step(lengths[n], *args)

        return run

    return lax.cond(longest <= lengths[0], branch(0), branch(1), *operands)


def step(length, student_hidden, head_weight, teacher_logprobs, align_index, align_tiles, grad_scale, tab):
    vocab = lax.axis_size("vocab")
    dp = lax.axis_size("dp")
    v = lax.axis_index("vocab")
    d = lax.axis_index("dp")
    chips, c = dp // 2, d % 2
    core = c.astype(jnp.int32)[None]
    tokens, features = student_hidden.shape
    count = teacher_logprobs.shape[1] // BLOCK
    pairs = align_tiles.shape[0] * K
    groups = [[2 * i + j for i in range(chips)] for j in range(2)]

    capacity = (2 * pairs + vocab - 1) // vocab
    lengths = [length if t >= vocab // 2 else capacity for t in range(1, vocab)]
    blocks, sources = [], []
    for n in range(HALVES):
        own, *lists = teacher_lists(n, tab, teacher_logprobs, lengths)
        got = []
        for t in range(1, vocab):
            got.append(swap(lists[t - 1], "vocab", t))
        blocks.append(own)
        sources.append([own] + got)

    weight_own = lax.all_to_all(head_weight, "dp", split_axis=1, concat_axis=0, axis_index_groups=groups, tiled=True)
    weight_other = swap(weight_own, "dp", 1)

    hidden = student_hidden.reshape(tokens, chips, 2, features // dp).transpose(2, 0, 1, 3)
    hidden = lax.optimization_barrier(hidden.reshape(2, tokens, features // 2))
    others = [swap(hidden, "dp", 2 * j) for j in range(1, chips)]
    order = list(range(chips))[::-1]
    hidden = jnp.concatenate(others[::-1] + [hidden], axis=1)
    e, local = logits_parts(core, hidden, weight_own, weight_other, tokens)

    row_sums = jnp.sum(align_tiles.astype(F32), axis=3).reshape(pairs, BLOCK)
    all_sums = [row_sums] + [swap(row_sums, "vocab", t) for t in range(1, vocab)]
    rows = align_index.reshape(vocab, pairs)
    all_rows = [lax.dynamic_index_in_dim(rows, v ^ t, 0, keepdims=False) for t in range(vocab)]
    hits = (jnp.concatenate(all_rows)[None, :] == (v * count + jnp.arange(count))[:, None]).astype(F32)
    entry_weight = jnp.dot(hits, jnp.concatenate(all_sums), precision=lax.Precision.HIGHEST)
    mass = jnp.concatenate(
        [jnp.sum(part.astype(F32) * entry_weight[:, None, :], axis=(0, 2)) for part in blocks]
    )

    share = jnp.concatenate([local.reshape(2 * chips, tokens), mass[None]])
    shares = [share] + [swap(share, "vocab", t) for t in range(1, vocab)]
    plane_top = functools.reduce(jnp.maximum, [s[:chips] for s in shares])
    plane_total = sum(s[chips : 2 * chips] * jnp.exp(s[:chips] - plane_top) for s in shares)
    plane_mass = sum(s[2 * chips] for s in shares)
    share = jnp.concatenate([plane_top, plane_total, plane_mass[None], grad_scale[None]])
    shares = [share] + [swap(share, "dp", 2 * j) for j in range(1, chips)]
    column = jax.ShapeDtypeStruct((chips, tokens, 1), F32)
    a, b = pl.pallas_call(
        functools.partial(stats_kernel, order),
        in_specs=[VMEM] * (chips + 1),
        out_specs=[VMEM, VMEM],
        out_shape=[column, column],
        name="stats",
    )(local, *shares)

    columns = []
    for n in range(HALVES):
        parts = mapped_parts(tab, sources[n], align_tiles, order)
        columns += [x if j == 0 else swap(x, "dp", 2 * j) for x, j in zip(parts, order)]
    dl, *terms = grads(core, e, a, b, weight_own, weight_other, columns)
    terms = [x if j == 0 else swap(x, "dp", 2 * j) for x, j in zip(terms, order)]
    rows_sum = sum([x.astype(F32) for x in terms[:-1]], terms[-1].astype(F32))
    rows_sum = rows_sum.astype(BF16).reshape(2, tokens, chips, features // dp).transpose(1, 2, 0, 3)
    pieces = rows_sum.reshape(tokens, vocab, features // vocab).transpose(1, 0, 2)
    piece = lambda t: lax.dynamic_index_in_dim(pieces, v ^ t, 0, keepdims=False)
    hidden_grad = piece(0).astype(F32)
    others = [swap(piece(t), "vocab", t) for t in range(1, vocab)]
    hidden_grad = sum([x.astype(F32) for x in others], hidden_grad).astype(BF16)
    dl = dl.reshape(chips * tokens, -1)

    def head_half(half):
        x = lax.dynamic_index_in_dim(hidden, half, 0, keepdims=False)
        return lax.dot_general(x, dl, (((0,), (0,)), ((), ())), preferred_element_type=F32).astype(BF16)

    half = head_half(1 - c)
    got = swap(half, "dp", 1)
    half = head_half(c)
    head_terms = (half.astype(F32) + got.astype(F32)).astype(BF16)
    head_grad = lax.all_to_all(
        head_terms, "dp", split_axis=0, concat_axis=1, axis_index_groups=groups, tiled=True
    )
    return (hidden_grad, head_grad)


def solution(mesh):
    placed = (
        P("dp", None),
        P("dp", "vocab"),
        P("dp", "vocab"),
        P(),
        P("vocab", None, None, None),
        P("dp"),
    )
    return jax.shard_map(
        body,
        mesh=mesh,
        in_specs=placed,
        out_specs=(P("dp", "vocab"), P("dp", "vocab")),
        check_vma=False,
    )
```

```python
import functools

import jax
import jax.numpy as jnp
from jax import lax
from jax.experimental import pallas as pl
from jax.experimental.pallas import tpu as pltpu
from jax.sharding import PartitionSpec as P


BLOCK = 128
K = 2
SPLIT = (64, 64)
HALVES = len(SPLIT)

ANY = pl.BlockSpec(memory_space=pl.ANY)
VMEM = pl.BlockSpec(memory_space=pltpu.VMEM)
F32 = jnp.float32
BF16 = jnp.bfloat16


def swap(x, axis, bits):
    return lax.ppermute(x, axis, [(i, i ^ bits) for i in range(lax.axis_size(axis))])


def parts_of(tokens):
    return [tokens * sum(SPLIT[:n]) // sum(SPLIT) for n in range(HALVES + 1)]


def probs_kernel(tab_ref, x_ref, own_ref, *out_refs):
    def convert(block, carry):
        columns = pl.ds(pl.multiple_of(block * BLOCK, BLOCK), BLOCK)
        own_ref[block] = jnp.exp(x_ref[:, columns]).astype(BF16)
        return carry

    lax.fori_loop(0, own_ref.shape[0], convert, 0, unroll=4)
    for t, out in enumerate(out_refs):

        def copy(slot, carry, t=t, out=out):
            out[slot] = own_ref[tab_ref[3 + t, slot]]
            return carry

        lax.fori_loop(0, out.shape[0], copy, 0, unroll=4)


def teacher_lists(part, tab, logprobs, lengths):
    tokens, cols = logprobs.shape
    ends = parts_of(tokens)
    rows = ends[part + 1] - ends[part]
    shapes = [(n, rows, BLOCK) for n in [cols // BLOCK] + lengths]
    whole = lambda shape: pl.BlockSpec(shape, lambda i, tab: (0, 0, 0))
    return pl.pallas_call(
        probs_kernel,
        grid_spec=pltpu.PrefetchScalarGridSpec(
            num_scalar_prefetch=1,
            grid=(1,),
            in_specs=[pl.BlockSpec((rows, cols), lambda i, tab: (ends[part] // rows, 0))],
            out_specs=[whole(shape) for shape in shapes],
        ),
        out_shape=[jax.ShapeDtypeStruct(shape, BF16) for shape in shapes],
        name="probs",
    )(tab, logprobs)


def mapped_kernel(pieces, tab_ref, *refs):
    sources, tiles_ref, outs = refs[: -len(pieces) - 3], refs[-len(pieces) - 3], refs[-len(pieces) - 2 : -2]
    buf, sem = refs[-2], refs[-1]
    me = tab_ref[2, 0]
    per = outs[0].shape[1] // BLOCK

    def start(p, carry):
        source, block = tab_ref[0, p], tab_ref[1, p]
        for i, ref in enumerate(sources):

            @pl.when(source == i)
            def _(ref=ref):
                pltpu.make_async_copy(ref.at[block], buf.at[p], sem).start()

        return carry

    lax.fori_loop(0, buf.shape[0], start, 0)
    pltpu.make_async_copy(buf, buf, sem).wait()
    for piece, out in zip(pieces, outs):
        dest = lax.bitwise_xor(me, piece)
        for j in range(per):
            b = dest * per + j
            total = jnp.dot(buf[K * b], tiles_ref[b, 0], preferred_element_type=F32)
            for k in range(1, K):
                total += jnp.dot(buf[K * b + k], tiles_ref[b, k], preferred_element_type=F32)
            out[:, j * BLOCK : (j + 1) * BLOCK] = total.astype(BF16)


def mapped_parts(tab, sources, tiles, pieces):
    rows = sources[0].shape[1]
    cols = tiles.shape[0] * BLOCK // len(pieces)
    return pl.pallas_call(
        functools.partial(mapped_kernel, pieces),
        grid_spec=pltpu.PrefetchScalarGridSpec(
            num_scalar_prefetch=1,
            grid=(),
            in_specs=[ANY] * len(sources) + [VMEM],
            out_specs=[VMEM] * len(pieces),
            scratch_shapes=[pltpu.VMEM((tab.shape[1], rows, BLOCK), BF16), pltpu.SemaphoreType.DMA],
        ),
        out_shape=[jax.ShapeDtypeStruct((rows, cols), BF16)] * len(pieces),
        name="mapped",
    )(tab, *sources, tiles)


def turned(x):
    n = max(x.shape)
    full = jnp.broadcast_to(x, (n, n)).T
    return full[:, :1] if x.shape[0] == 1 else full[:1]


def logits_kernel(core_ref, x_ref, own_ref, other_ref, e_ref, s_ref):
    i, c = pl.program_id(0), core_ref[0]
    logits = jnp.dot(x_ref[c], own_ref[...], preferred_element_type=F32)
    logits += jnp.dot(x_ref[1 - c], other_ref[...], preferred_element_type=F32)
    top = jnp.max(logits, axis=1, keepdims=True)
    e = jnp.exp(logits - top)
    e_ref[0] = e
    s_ref[0, pl.ds(i, 1)] = turned(top)
    s_ref[1, pl.ds(i, 1)] = turned(jnp.sum(e, axis=1, keepdims=True))


def logits_parts(core, hidden, own, other, tokens):
    chips = hidden.shape[1] // tokens
    features, cols = own.shape
    fixed = pl.BlockSpec((features, cols), lambda i, core: (0, 0))
    return pl.pallas_call(
        logits_kernel,
        grid_spec=pltpu.PrefetchScalarGridSpec(
            num_scalar_prefetch=1,
            grid=(chips,),
            in_specs=[pl.BlockSpec((2, tokens, features), lambda i, core: (0, i, 0)), fixed, fixed],
            out_specs=[
                pl.BlockSpec((1, tokens, cols), lambda i, core: (i, 0, 0)),
                pl.BlockSpec((2, chips, tokens), lambda i, core: (0, 0, 0)),
            ],
        ),
        out_shape=[
            jax.ShapeDtypeStruct((chips, tokens, cols), F32),
            jax.ShapeDtypeStruct((2, chips, tokens), F32),
        ],
        name="logits",
    )(core, hidden, own, other)


def stats_kernel(order, own_ref, *refs):
    shares, a_ref, b_ref = refs[:-2], refs[-2], refs[-1]
    chips = len(shares)
    for k, piece in enumerate(order):
        rows = [order.index(piece ^ r) for r in range(chips)]
        tops = [shares[r][j : j + 1] for r, j in enumerate(rows)]
        top = functools.reduce(jnp.maximum, tops)
        total = sum(shares[r][chips + j : chips + j + 1] * jnp.exp(tops[r] - top) for r, j in enumerate(rows))
        mass = shares[piece][2 * chips : 2 * chips + 1]
        scale = shares[piece][2 * chips + 1 : 2 * chips + 2]
        a_ref[k] = turned(scale * mass * (jnp.exp(own_ref[0, k : k + 1] - top) / total))
        b_ref[k] = turned(scale)


def grads_kernel(core_ref, e_ref, a_ref, b_ref, own_ref, other_ref, *refs):
    count, tokens = e_ref.shape[:2]
    mapped, dl_ref, outs = refs[: HALVES * count], refs[-count - 1], refs[-count:]
    ends = parts_of(tokens)
    c = core_ref[0]
    for n in range(HALVES):
        some = slice(ends[n], ends[n + 1])
        for k in range(count):
            columns = mapped[n * count + k][...].astype(F32)
            dl_ref[k, some] = (a_ref[k, some] * e_ref[k, some] - b_ref[k, some] * columns).astype(BF16)
    dl = dl_ref[...].reshape(count * tokens, -1)
    for half, weight in ((c, own_ref), (1 - c, other_ref)):
        terms = lax.dot_general(dl, weight[...], (((1,), (1,)), ((), ())), preferred_element_type=F32)
        for k in range(count):
            outs[k][half] = terms[k * tokens : (k + 1) * tokens].astype(BF16)


def grads(core, e, a, b, own, other, mapped):
    count, tokens = e.shape[:2]
    return pl.pallas_call(
        grads_kernel,
        grid_spec=pltpu.PrefetchScalarGridSpec(
            num_scalar_prefetch=1,
            grid=(),
            in_specs=[VMEM] * (5 + len(mapped)),
            out_specs=[VMEM] * (1 + count),
        ),
        out_shape=[jax.ShapeDtypeStruct(e.shape, BF16)]
        + [jax.ShapeDtypeStruct((2, tokens, own.shape[0]), BF16)] * count,
        name="grads",
    )(core, e, a, b, own, other, *mapped)


def sum_kernel(*refs):
    total = refs[0][...].astype(F32)
    for ref in refs[1:-1]:
        total += ref[...].astype(F32)
    refs[-1][...] = total.astype(BF16)


def plan(align_index, pairs, count, chip):
    vocab = lax.axis_size("vocab")
    v = lax.axis_index("vocab")
    rows = align_index.reshape(vocab, pairs)
    owner, local = lax.div(rows, jnp.int32(count)), lax.rem(rows, jnp.int32(count))
    number = jnp.arange(pairs)
    same = rows[:, :, None] == rows[:, None, :]
    first = ~jnp.any(same & (number[None, None, :] < number[None, :, None]), axis=2)
    less = (owner[:, :, None] == owner[:, None, :]) & (rows[:, None, :] < rows[:, :, None]) & first[:, None, :]
    rank = jnp.sum(less.astype(jnp.int32), axis=2)
    here = jnp.arange(vocab)[:, None]
    longest = jnp.max(jnp.where((owner ^ here) >= vocab // 2, rank + 1, 0))
    pick = lambda x, i: lax.dynamic_index_in_dim(x, i, 0, keepdims=False)
    own_owner = pick(owner, v)
    source = own_owner ^ v
    place = jnp.where(own_owner == v, pick(local, v), pick(rank, v))
    asked = (owner == v)[:, None, :] & (rank[:, None, :] == number[None, :, None]) & first[:, None, :]
    lists = jnp.sum(jnp.where(asked, local[:, None, :], 0), axis=2)
    mine = jnp.where(number == 0, chip, 0)
    tab = jnp.stack([source, place, mine] + [pick(lists, v ^ t) for t in range(1, vocab)])
    return tab.astype(jnp.int32), longest


def body(student_hidden, head_weight, teacher_logprobs, align_index, align_tiles, grad_scale):
    vocab = lax.axis_size("vocab")
    chips = lax.axis_size("dp") // 2
    count = teacher_logprobs.shape[1] // BLOCK
    pairs = align_tiles.shape[0] * K
    capacity = (2 * pairs + vocab - 1) // vocab
    if vocab & (vocab - 1) or chips & (chips - 1):
        raise ValueError("mesh sizes")
    tab, longest = plan(align_index, pairs, count, lax.axis_index("dp") // 2)
    operands = (student_hidden, head_weight, teacher_logprobs, align_index, align_tiles, grad_scale, tab)
    lengths = (11 * capacity // 16, capacity)

    def branch(n):
        def run(*args):
            return step(lengths[n], *args)

        return run

    return lax.cond(longest <= lengths[0], branch(0), branch(1), *operands)


def step(length, student_hidden, head_weight, teacher_logprobs, align_index, align_tiles, grad_scale, tab):
    vocab = lax.axis_size("vocab")
    dp = lax.axis_size("dp")
    v = lax.axis_index("vocab")
    d = lax.axis_index("dp")
    chips, c = dp // 2, d % 2
    core = c.astype(jnp.int32)[None]
    tokens, features = student_hidden.shape
    count = teacher_logprobs.shape[1] // BLOCK
    pairs = align_tiles.shape[0] * K
    groups = [[2 * i + j for i in range(chips)] for j in range(2)]

    capacity = (2 * pairs + vocab - 1) // vocab
    lengths = [length if t >= vocab // 2 else capacity for t in range(1, vocab)]
    blocks, sources = [], []
    for n in range(HALVES):
        own, *lists = teacher_lists(n, tab, teacher_logprobs, lengths)
        got = []
        for t in range(1, vocab):
            got.append(swap(lists[t - 1], "vocab", t))
        blocks.append(own)
        sources.append([own] + got)

    weight_own = lax.all_to_all(head_weight, "dp", split_axis=1, concat_axis=0, axis_index_groups=groups, tiled=True)
    weight_other = swap(weight_own, "dp", 1)

    hidden = student_hidden.reshape(tokens, chips, 2, features // dp).transpose(2, 0, 1, 3)
    hidden = lax.optimization_barrier(hidden.reshape(2, tokens, features // 2))
    others = [swap(hidden, "dp", 2 * j) for j in range(1, chips)]
    order = list(range(chips))[::-1]
    hidden = jnp.concatenate(others[::-1] + [hidden], axis=1)
    e, local = logits_parts(core, hidden, weight_own, weight_other, tokens)

    row_sums = jnp.sum(align_tiles.astype(F32), axis=3).reshape(pairs, BLOCK)
    all_sums = [row_sums] + [swap(row_sums, "vocab", t) for t in range(1, vocab)]
    rows = align_index.reshape(vocab, pairs)
    all_rows = [lax.dynamic_index_in_dim(rows, v ^ t, 0, keepdims=False) for t in range(vocab)]
    hits = (jnp.concatenate(all_rows)[None, :] == (v * count + jnp.arange(count))[:, None]).astype(F32)
    entry_weight = jnp.dot(hits, jnp.concatenate(all_sums), precision=lax.Precision.HIGHEST)
    mass = jnp.concatenate(
        [jnp.sum(part.astype(F32) * entry_weight[:, None, :], axis=(0, 2)) for part in blocks]
    )

    share = jnp.concatenate([local.reshape(2 * chips, tokens), mass[None]])
    shares = [share] + [swap(share, "vocab", t) for t in range(1, vocab)]
    plane_top = functools.reduce(jnp.maximum, [s[:chips] for s in shares])
    plane_total = sum(s[chips : 2 * chips] * jnp.exp(s[:chips] - plane_top) for s in shares)
    plane_mass = sum(s[2 * chips] for s in shares)
    share = jnp.concatenate([plane_top, plane_total, plane_mass[None], grad_scale[None]])
    shares = [share] + [swap(share, "dp", 2 * j) for j in range(1, chips)]
    column = jax.ShapeDtypeStruct((chips, tokens, 1), F32)
    a, b = pl.pallas_call(
        functools.partial(stats_kernel, order),
        in_specs=[VMEM] * (chips + 1),
        out_specs=[VMEM, VMEM],
        out_shape=[column, column],
        name="stats",
    )(local, *shares)

    columns = []
    for n in range(HALVES):
        parts = mapped_parts(tab, sources[n], align_tiles, order)
        columns += [x if j == 0 else swap(x, "dp", 2 * j) for x, j in zip(parts, order)]
    dl, *terms = grads(core, e, a, b, weight_own, weight_other, columns)
    terms = [x if j == 0 else swap(x, "dp", 2 * j) for x, j in zip(terms, order)]
    rows_sum = sum([x.astype(F32) for x in terms[:-1]], terms[-1].astype(F32))
    rows_sum = rows_sum.astype(BF16).reshape(2, tokens, chips, features // dp).transpose(1, 2, 0, 3)
    pieces = rows_sum.reshape(tokens, vocab, features // vocab).transpose(1, 0, 2)
    piece = lambda t: lax.dynamic_index_in_dim(pieces, v ^ t, 0, keepdims=False)
    others = [swap(piece(t), "vocab", t) for t in range(1, vocab)]
    hidden_grad = pl.pallas_call(
        sum_kernel,
        in_specs=[VMEM] * vocab,
        out_specs=VMEM,
        out_shape=jax.ShapeDtypeStruct(others[0].shape, BF16),
        name="hidden_sum",
    )(piece(0), *others)
    dl = dl.reshape(chips * tokens, -1)

    def head_half(half):
        x = lax.dynamic_index_in_dim(hidden, half, 0, keepdims=False)
        return lax.dot_general(x, dl, (((0,), (0,)), ((), ())), preferred_element_type=F32).astype(BF16)

    half = head_half(1 - c)
    got = swap(half, "dp", 1)
    half = head_half(c)
    head_terms = (half.astype(F32) + got.astype(F32)).astype(BF16)
    head_grad = lax.all_to_all(
        head_terms, "dp", split_axis=0, concat_axis=1, axis_index_groups=groups, tiled=True
    )
    return (hidden_grad, head_grad)


def solution(mesh):
    placed = (
        P("dp", None),
        P("dp", "vocab"),
        P("dp", "vocab"),
        P(),
        P("vocab", None, None, None),
        P("dp"),
    )
    return jax.shard_map(
        body,
        mesh=mesh,
        in_specs=placed,
        out_specs=(P("dp", "vocab"), P("dp", "vocab")),
        check_vma=False,
    )
```
